512 devices in a mesh: depth: 16 (over z), rows: 32 (over y, x, core).
Axes of the slice: x: 4, y: 4, z: 16, core: 2. Of those that a mesh axis runs over, the one named last changes fastest.
Arguments:
- node_feat: bfloat16 [512, 32768], P('depth', 'rows'), may hold values from -6 to 6
- grad_out: bfloat16 [512, 32768], P('depth', 'rows'), may hold values from -0.25 to 0.25
- adjacency: bfloat16 [512, 256, 256], P('rows'), may hold values from -0.1875 to 0.1875
- tile_count: int32 [32], replicated, may hold values from 4 to 16, as said below
- tile_row: int32 [32, 16], replicated, may hold values from 0 to 3, as said below
- tile_col: int32 [32, 16], replicated, may hold values from 0 to 127, as said below
Outputs:
- weight_grad: float32 [32, 16, 256, 256], P('rows', 'depth')
The draws below stay inside these ranges and needn't reach their ends.
Inputs may be any that keep to these rules, and one draw needn't show every extreme that they name: `tile_count`: the number of live slots of each owner; one owner has exactly 16 in every draw. `tile_row`: 0 in dead slots. `tile_col`: 0 in dead slots. An owner's live slots name distinct column tiles; at most 2 of them lie among the node tiles of any one owner (column tile // 4), and every owner has exactly 2 from some owner.
All inputs are finite; a program needn't handle non-finite values.
Results may differ from the reference program's by a relative error of at most 0.0029.
Values may be sent and summed in bfloat16 or wider, within the bound.
No kernel may reach another device: no remote copies, remote signals or barrier semaphores. Data moves between devices by JAX's collectives and lax.ppermute only.
A program may use at most 64 MiB of HBM per device.

```python
import jax
import jax.numpy as jnp
from jax import lax

TILE = 256
FEAT = 512
TROWS_DEV = 4
PAIR_MOST = 2
SLOTS = 16
NTILES = 128
NODES = 32768
N_DEPTH = 16
N_ROWS = 32


def tile_layout(key):
    counts = jax.random.randint(jax.random.fold_in(key, 11), (N_ROWS,), SLOTS // 4, 3 * SLOTS // 4 + 1)
    busiest = jax.random.randint(jax.random.fold_in(key, 12), (), 0, N_ROWS)
    owner_ids = jnp.arange(N_ROWS, dtype=jnp.int32)
    counts = jnp.where(owner_ids == busiest, SLOTS, counts).astype(jnp.int32)
    scores = jax.random.randint(jax.random.fold_in(key, 13), (N_ROWS, N_ROWS), 1, 1 << 16) * N_ROWS
    scores = scores + owner_ids[None, :]
    forced = (owner_ids[:, None] == busiest) & (owner_ids[None, :] == N_ROWS - 1)
    scores = jnp.where(forced, 0, scores)
    owner_order = jnp.argsort(scores, axis=1).astype(jnp.int32)
    slot_ids = jnp.arange(SLOTS, dtype=jnp.int32)
    leading = slot_ids < PAIR_MOST
    remaining = jnp.maximum(slot_ids - PAIR_MOST, 0)
    rank_of = jnp.where(leading, slot_ids, remaining // (N_ROWS - 1))
    pick_index = jnp.where(leading, 0, 1 + remaining % (N_ROWS - 1))
    owners = jnp.take_along_axis(owner_order, jnp.broadcast_to(pick_index[None, :], (N_ROWS, SLOTS)), axis=1)
    offsets = jax.random.randint(jax.random.fold_in(key, 14), (N_ROWS, N_ROWS), 0, TROWS_DEV)
    offsets = jnp.where(forced, TROWS_DEV - 1, offsets)
    offsets_here = jnp.take_along_axis(offsets, owners, axis=1)
    columns = owners * TROWS_DEV + (offsets_here + rank_of[None, :]) % TROWS_DEV
    row_ids = jax.random.randint(jax.random.fold_in(key, 15), (N_ROWS, SLOTS), 0, TROWS_DEV)
    first_busy = (owner_ids[:, None] == busiest) & (slot_ids[None, :] == 0)
    row_ids = jnp.where(first_busy, TROWS_DEV - 1, row_ids)
    is_live = slot_ids[None, :] < counts[:, None]
    columns = jnp.where(is_live, columns, 0).astype(jnp.int32)
    row_ids = jnp.where(is_live, row_ids, 0).astype(jnp.int32)
    return (counts, row_ids, columns)


def draw_tile_count(key, part):
    return tile_layout(key)[0]


def draw_tile_row(key, part):
    return tile_layout(key)[1]


def draw_tile_col(key, part):
    return tile_layout(key)[2]


def block_scale(stream_key, shape, cuts, smallest, top_value):
    level = 1.0
    for position, shards_of in cuts:
        steps = jax.random.uniform(jax.random.fold_in(jax.random.fold_in(stream_key, 6), position), (shards_of,), jnp.float32, smallest / len(cuts), top_value / len(cuts))
        level = level * jnp.repeat(jnp.exp(steps), shape[position] // shards_of).reshape((-1,) + (1,) * (len(shape) - 1 - position))
    return level


def gaussian(rng, extent, width, most, shards=(), held_as=jnp.bfloat16):
    drawn = jax.random.normal(rng, extent, jnp.float32) * width
    if len(shards) > 0:
        drawn = block_scale(rng, extent, shards, -0.22, 0.18) * drawn
    return jnp.clip(drawn, min=-most, max=most).astype(held_as)


def setup_inputs(seed: int = 0) -> dict:
    streams_of = jax.random.split(jax.random.key(seed), 7)
    node_feat = gaussian(streams_of[0], (FEAT, NODES), 1.0, 6.0, ((0, 16), (1, 32)))
    grad_out = gaussian(streams_of[1], (FEAT, NODES), FEAT ** -0.5, 0.25, ((0, 16), (1, 32)))
    adjacency = gaussian(streams_of[2], (N_ROWS * SLOTS, TILE, TILE), (4 * TILE) ** -0.5, 0.1875, ((0, 32),))
    tile_count = draw_tile_count(jax.random.fold_in(streams_of[6], 71), 0)
    tile_row = draw_tile_row(jax.random.fold_in(streams_of[6], 71), 0)
    tile_col = draw_tile_col(jax.random.fold_in(streams_of[6], 71), 0)
    return dict(node_feat=node_feat, grad_out=grad_out, adjacency=adjacency, tile_count=tile_count, tile_row=tile_row, tile_col=tile_col)


top_precision = lax.Precision.HIGHEST


def reference(node_feat, grad_out, adjacency, tile_count, tile_row, tile_col):
    feat_tiles = node_feat.astype(jnp.float32).reshape(FEAT, NTILES, TILE)
    grad_tiles = grad_out.astype(jnp.float32).reshape(FEAT, NTILES, TILE)
    owner_tiles = adjacency.astype(jnp.float32).reshape(N_ROWS, SLOTS, TILE, TILE)
    slot_ids = jnp.arange(SLOTS, dtype=jnp.int32)
    is_live = (slot_ids[None, :] < tile_count[:, None]).astype(jnp.float32)
    global_rows = (jnp.arange(N_ROWS, dtype=jnp.int32)[:, None] * TROWS_DEV + tile_row).astype(jnp.int32)
    global_cols = tile_col.astype(jnp.int32)

    def accumulate(running, inputs):
        summed_h, summed_g = running
        tiles_here, rows_here, cols_here, live_here = inputs
        weights = tiles_here * live_here[:, None, None]
        h_terms = jnp.einsum("fsb,sab->fsa", feat_tiles[:, cols_here], weights, precision=top_precision)
        g_terms = jnp.einsum("fsa,sab->fsb", grad_tiles[:, rows_here], weights, precision=top_precision)
        return (summed_h.at[:, rows_here].add(h_terms), summed_g.at[:, cols_here].add(g_terms)), None

    zero_field = jnp.zeros((FEAT, NTILES, TILE), jnp.float32)
    totals, unused = lax.scan(accumulate, (zero_field, zero_field), (owner_tiles, global_rows, global_cols, is_live))
    h_round = lax.optimization_barrier(totals[0].astype(jnp.bfloat16)).astype(jnp.float32)
    g_round = lax.optimization_barrier(totals[1].astype(jnp.bfloat16)).astype(jnp.float32)
    group_size = FEAT // N_DEPTH

    def tile_grads(inputs):
        rows_here, cols_here, live_here = inputs
        dy_rows = grad_tiles[:, rows_here].reshape(N_DEPTH, group_size, SLOTS, TILE)
        g_rows = g_round[:, rows_here].reshape(N_DEPTH, group_size, SLOTS, TILE)
        h_cols = h_round[:, cols_here].reshape(N_DEPTH, group_size, SLOTS, TILE)
        x_cols = feat_tiles[:, cols_here].reshape(N_DEPTH, group_size, SLOTS, TILE)
        parts = jnp.einsum("qfsa,qfsb->qsab", dy_rows, h_cols, precision=top_precision)
        parts = parts + jnp.einsum("qfsa,qfsb->qsab", g_rows, x_cols, precision=top_precision)
        return jnp.sum(parts, axis=0) * live_here[:, None, None]

    return lax.map(tile_grads, (global_rows, global_cols, is_live))
```

```python
import jax
import jax.numpy as jnp
from jax import lax
from jax.experimental import pallas as pl
from jax.experimental.pallas import tpu as pltpu
from jax.sharding import PartitionSpec as P

PAIR_MOST = 2
SMEM = pltpu.SMEM
VMEM = pltpu.VMEM


def spec_of(space):
    return pl.BlockSpec(memory_space=space)


def request_tables(tile_row, tile_col, tile_count, row_tiles, own_index):
    slot_count = tile_col.shape[1]
    slot_ids = jnp.arange(slot_count, dtype=jnp.int32)
    is_live = slot_ids[None, :] < tile_count[:, None]
    owners = tile_col // row_tiles
    wanted = is_live & (owners == own_index)
    code = tile_col % row_tiles + 1
    first = jnp.max(jnp.where(wanted, (slot_count - 1 - slot_ids)[None, :] * 8 + code, 0), axis=1)
    last = jnp.max(jnp.where(wanted, slot_ids[None, :] * 8 + code, 0), axis=1)
    two = (last // 8 + first // 8) != slot_count - 1
    asked = jnp.stack([first % 8, jnp.where(two, last % 8, 0)], axis=1).reshape(-1)
    my_owner = lax.dynamic_index_in_dim(owners, own_index, 0, keepdims=False)
    my_live = lax.dynamic_index_in_dim(is_live, own_index, 0, keepdims=False)
    my_row = lax.dynamic_index_in_dim(tile_row, own_index, 0, keepdims=False)
    earlier = (slot_ids[:, None] > slot_ids[None, :]) & (my_owner[:, None] == my_owner[None, :])
    rank = jnp.sum(earlier.astype(jnp.int32), axis=1)
    place = jnp.where(my_live, my_owner * PAIR_MOST + rank, -1)
    return asked, jnp.concatenate([place, my_row])


def tile_cols(index, width):
    return pl.ds(pl.multiple_of(index * width, width), width)


def pack_x_kernel(asked_ref, x_ref, out_ref):
    width = out_ref.shape[2]
    for p in range(out_ref.shape[0]):
        t = jnp.maximum(asked_ref[p] - 1, 0)
        out_ref[p] = x_ref[:, tile_cols(t, width)]


def g_terms_kernel(mine_ref, dy_ref, a_ref, g_ref, dyz_ref):
    slots, width = a_ref.shape[0], a_ref.shape[1]
    g_ref[...] = jnp.zeros(g_ref.shape, g_ref.dtype)
    for s in range(slots):
        place = mine_ref[s]
        dy = dy_ref[:, tile_cols(mine_ref[slots + s], width)]
        dyz_ref[s] = dy
        term = jnp.dot(dy, a_ref[s], preferred_element_type=jnp.float32).astype(g_ref.dtype)

        @pl.when(place >= 0)
        def _():
            g_ref[jnp.maximum(place, 0)] = term


def h_kernel(mine_ref, asked_ref, xin_ref, a_ref, h_ref, xz_ref, acc_ref):
    slots = a_ref.shape[0]
    acc_ref[...] = jnp.zeros(acc_ref.shape, acc_ref.dtype)
    for s in range(slots):
        place = mine_ref[s]
        row = mine_ref[slots + s]
        x = xin_ref[jnp.maximum(place, 0)]
        xz_ref[s] = x
        term = lax.dot_general(x, a_ref[s], (((1,), (1,)), ((), ())), preferred_element_type=jnp.float32)

        @pl.when(place >= 0)
        def _():
            acc_ref[row] += term

    for p in range(h_ref.shape[0]):
        t = jnp.maximum(asked_ref[p] - 1, 0)
        h_ref[p] = acc_ref[t].astype(h_ref.dtype)


def g_sum_kernel(mine_ref, asked_ref, gin_ref, gz_ref, acc_ref):
    acc_ref[...] = jnp.zeros(acc_ref.shape, acc_ref.dtype)
    for p in range(gin_ref.shape[0]):
        t = asked_ref[p]

        @pl.when(t > 0)
        def _():
            acc_ref[jnp.maximum(t - 1, 0)] += gin_ref[p].astype(jnp.float32)

    slots = gz_ref.shape[0]
    for s in range(slots):
        gz_ref[s] = acc_ref[mine_ref[slots + s]].astype(gz_ref.dtype)


def pick_kernel(mine_ref, hin_ref, hz_ref):
    for s in range(hz_ref.shape[0]):
        hz_ref[s] = hin_ref[jnp.maximum(mine_ref[s], 0)]


def body(node_feat, grad_out, adjacency, tile_count, tile_row, tile_col):
    slots, width = adjacency.shape[0], adjacency.shape[1]
    feat_part = node_feat.shape[0]
    row_tiles = node_feat.shape[1] // width
    own_index = lax.axis_index("rows")
    places = lax.axis_size("rows") * PAIR_MOST
    bf16 = node_feat.dtype
    asked, mine = request_tables(tile_row, tile_col, tile_count, row_tiles, own_index)
    packed = jax.ShapeDtypeStruct((places, feat_part, width), bf16)
    slotted = jax.ShapeDtypeStruct((slots, feat_part, width), bf16)
    acc = VMEM((row_tiles, feat_part, width), jnp.float32)
    smem, vmem = spec_of(SMEM), spec_of(VMEM)

    x_out = pl.pallas_call(pack_x_kernel, out_shape=packed, in_specs=[smem, vmem], out_specs=vmem)(asked, node_feat)
    x_in = lax.all_to_all(x_out, "rows", 0, 0, tiled=True)
    g_out, dy_z = pl.pallas_call(
        g_terms_kernel, out_shape=(packed, slotted), in_specs=[smem, vmem, vmem], out_specs=(vmem, vmem)
    )(mine, grad_out, adjacency)
    g_in = lax.all_to_all(g_out, "rows", 0, 0, tiled=True)
    h_out, x_z = pl.pallas_call(
        h_kernel,
        out_shape=(packed, slotted),
        in_specs=[smem, smem, vmem, vmem],
        out_specs=(vmem, vmem),
        scratch_shapes=[acc],
    )(mine, asked, x_in, adjacency)
    h_in = lax.all_to_all(h_out, "rows", 0, 0, tiled=True)
    g_z = pl.pallas_call(
        g_sum_kernel, out_shape=slotted, in_specs=[smem, smem, vmem], out_specs=vmem, scratch_shapes=[acc]
    )(mine, asked, g_in)
    h_z = pl.pallas_call(pick_kernel, out_shape=slotted, in_specs=[smem, vmem], out_specs=vmem)(mine, h_in)
    left = jnp.concatenate([dy_z, g_z], axis=1)
    right = jnp.concatenate([h_z, x_z], axis=1)
    both = jnp.concatenate([left, right], axis=1)
    full = lax.all_to_all(both, "depth", 0, 0, tiled=True)
    two = 2 * feat_part
    result = jnp.einsum("qfa,qfb->ab", full[:, :two], full[:, two:], preferred_element_type=jnp.float32)
    alive = lax.axis_index("depth") < lax.dynamic_index_in_dim(tile_count, own_index, 0, keepdims=False)
    return jnp.where(alive, result, 0.0)[None, None]


def solution(mesh):
    in_specs = (P("depth", "rows"), P("depth", "rows"), P("rows", None, None), P(), P(), P())
    out_specs = P("rows", "depth", None, None)
    return jax.shard_map(body, mesh=mesh, in_specs=in_specs, out_specs=out_specs, check_vma=False)
```

```python
import jax
import jax.numpy as jnp
from jax import lax
from jax.experimental import pallas as pl
from jax.experimental.pallas import tpu as pltpu
from jax.sharding import PartitionSpec as P

PAIR_MOST = 2
SMEM = pl.BlockSpec(memory_space=pltpu.SMEM)
VMEM = pl.BlockSpec(memory_space=pltpu.VMEM)
ANY = pl.BlockSpec(memory_space=pl.ANY)


def request_tables(tile_row, tile_col, tile_count, row_tiles, own_index):
    slot_count = tile_col.shape[1]
    slot_ids = jnp.arange(slot_count, dtype=jnp.int32)
    is_live = slot_ids[None, :] < tile_count[:, None]
    owners = tile_col // row_tiles
    wanted = is_live & (owners == own_index)
    code = tile_col % row_tiles + 1
    first = jnp.max(jnp.where(wanted, (slot_count - 1 - slot_ids)[None, :] * 8 + code, 0), axis=1)
    last = jnp.max(jnp.where(wanted, slot_ids[None, :] * 8 + code, 0), axis=1)
    two = (last // 8 + first // 8) != slot_count - 1
    asked = jnp.stack([first % 8, jnp.where(two, last % 8, 0)])
    my_owner = lax.dynamic_index_in_dim(owners, own_index, 0, keepdims=False)
    my_live = lax.dynamic_index_in_dim(is_live, own_index, 0, keepdims=False)
    my_row = lax.dynamic_index_in_dim(tile_row, own_index, 0, keepdims=False)
    earlier = (slot_ids[:, None] > slot_ids[None, :]) & (my_owner[:, None] == my_owner[None, :])
    rank = jnp.sum(earlier.astype(jnp.int32), axis=1)
    place = jnp.where(my_live, my_owner * PAIR_MOST + rank, -1)
    return asked, jnp.concatenate([place, my_row])


def tile_cols(index, width):
    return pl.ds(pl.multiple_of(index * width, width), width)


def send_xg_kernel(mine_ref, asked_ref, x_ref, dy_ref, a_ref, out_ref):
    slots, width = a_ref.shape[0], a_ref.shape[1]
    peers, most = out_ref.shape[0], out_ref.shape[1] // 2
    for r in range(peers):
        for k in range(most):
            t = jnp.maximum(asked_ref[k, r] - 1, 0)
            out_ref[r, k] = x_ref[:, tile_cols(t, width)]
            out_ref[r, most + k] = jnp.zeros(out_ref.shape[2:], out_ref.dtype)
    terms = []
    for s in range(slots):
        dy = dy_ref[:, tile_cols(mine_ref[slots + s], width)]
        terms.append(jnp.dot(dy, a_ref[s], preferred_element_type=jnp.float32).astype(out_ref.dtype))
    for s in range(slots):
        place = mine_ref[s]

        @pl.when(place >= 0)
        def _():
            out_ref[place // most, most + place % most] = terms[s]


def h_kernel(mine_ref, asked_ref, in_ref, a_ref, out_ref, a_buf, x_buf, acc_ref, a_sem, x_sem):
    slots = a_ref.shape[0]
    peers, most = out_ref.shape[0], out_ref.shape[1]
    row_tiles = acc_ref.shape[0]
    copies = []
    for s in range(slots):
        held = jnp.maximum(mine_ref[s], 0)
        x_copy = pltpu.make_async_copy(in_ref.at[held // most, held % most], x_buf.at[s], x_sem.at[s])
        a_copy = pltpu.make_async_copy(a_ref.at[s], a_buf.at[s], a_sem.at[s])
        x_copy.start()
        a_copy.start()
        copies.append((x_copy, a_copy))
    sums = [jnp.zeros(acc_ref.shape[1:], jnp.float32) for _ in range(row_tiles)]
    for s in range(slots):
        for copy in copies[s]:
            copy.wait()
        row = mine_ref[slots + s]
        term = lax.dot_general(
            x_buf[s], a_buf[s], (((1,), (1,)), ((), ())), preferred_element_type=jnp.float32
        )
        for t in range(row_tiles):
            sums[t] = sums[t] + jnp.where((row == t) & (mine_ref[s] >= 0), term, 0.0)
    for t in range(row_tiles):
        acc_ref[t] = sums[t].astype(acc_ref.dtype)
    for r in range(peers):
        for k in range(most):
            out_ref[r, k] = acc_ref[jnp.maximum(asked_ref[k, r] - 1, 0)]


def fill_kernel(mine_ref, asked_ref, in_ref, dy_ref, z_ref, acc_ref):
    peers, most = in_ref.shape[0], in_ref.shape[1] // 2
    slots, row_tiles = z_ref.shape[0], acc_ref.shape[0]
    feat, width = acc_ref.shape[1:]
    sums = [jnp.zeros(acc_ref.shape[1:], jnp.float32) for _ in range(row_tiles)]
    for r in range(peers):
        for k in range(most):
            term = in_ref[r, most + k].astype(jnp.float32)
            code = asked_ref[k, r]
            for t in range(row_tiles):
                sums[t] = sums[t] + jnp.where(code == t + 1, term, 0.0)
    for t in range(row_tiles):
        acc_ref[t] = sums[t].astype(acc_ref.dtype)
    for s in range(slots):
        held = jnp.maximum(mine_ref[s], 0)
        row = mine_ref[slots + s]
        z_ref[s, :feat] = dy_ref[:, tile_cols(row, width)]
        z_ref[s, feat : 2 * feat] = acc_ref[row]
        z_ref[s, 2 * feat : 3 * feat] = jnp.zeros((feat, width), z_ref.dtype)
        z_ref[s, 3 * feat :] = in_ref[held // most, held % most]


def add_h_kernel(mine_ref, in_ref, z_in_ref, z_ref, sem):
    del z_in_ref
    most, feat = in_ref.shape[1], in_ref.shape[2]
    copies = []
    for s in range(z_ref.shape[0]):
        held = jnp.maximum(mine_ref[s], 0)
        target = z_ref.at[s, pl.ds(2 * feat, feat)]
        copies.append(pltpu.make_async_copy(in_ref.at[held // most, held % most], target, sem.at[s]))
        copies[-1].start()
    for copy in copies:
        copy.wait()


def exchange(value, axis):
    return lax.all_to_all(value, axis, 0, 0, tiled=True)


def body(node_feat, grad_out, adjacency, tile_count, tile_row, tile_col):
    slots, width = adjacency.shape[0], adjacency.shape[1]
    feat = node_feat.shape[0]
    row_tiles = node_feat.shape[1] // width
    own_index = lax.axis_index("rows")
    depth_index = lax.axis_index("depth")
    peers = lax.axis_size("rows")
    bf16 = node_feat.dtype
    asked, mine = request_tables(tile_row, tile_col, tile_count, row_tiles, own_index)
    xg_type = jax.ShapeDtypeStruct((peers, 2 * PAIR_MOST, feat, width), bf16)
    h_type = jax.ShapeDtypeStruct((peers, PAIR_MOST, feat, width), bf16)
    z_type = jax.ShapeDtypeStruct((slots, 4 * feat, width), bf16)
    tiles = pltpu.VMEM((row_tiles, feat, width), bf16)
    sems = pltpu.SemaphoreType.DMA((slots,))

    xg_out = pl.pallas_call(
        send_xg_kernel, out_shape=xg_type, in_specs=[SMEM, SMEM, VMEM, VMEM, VMEM], out_specs=VMEM
    )(mine, asked, node_feat, grad_out, adjacency)
    xg_in = exchange(xg_out, "rows")
    h_out = pl.pallas_call(
        h_kernel,
        out_shape=h_type,
        in_specs=[SMEM, SMEM, ANY, ANY],
        out_specs=VMEM,
        scratch_shapes=[
            pltpu.VMEM(adjacency.shape, bf16),
            pltpu.VMEM((slots, feat, width), bf16),
            tiles,
            sems,
            sems,
        ],
    )(mine, asked, xg_in, adjacency)
    h_in = exchange(h_out, "rows")
    z_part = pl.pallas_call(
        fill_kernel,
        out_shape=z_type,
        in_specs=[SMEM, SMEM, VMEM, VMEM],
        out_specs=VMEM,
        scratch_shapes=[tiles],
    )(mine, asked, xg_in, grad_out)
    z_out = pl.pallas_call(
        add_h_kernel,
        out_shape=z_type,
        in_specs=[SMEM, ANY, ANY],
        out_specs=ANY,
        input_output_aliases={2: 0},
        scratch_shapes=[sems],
    )(mine, h_in, z_part)
    z_in = exchange(z_out, "depth")
    left, right = z_in[:, : 2 * feat], z_in[:, 2 * feat :]
    result = jnp.einsum("qfa,qfb->ab", left, right, preferred_element_type=jnp.float32)
    return jnp.where(mine[depth_index] >= 0, result, 0.0)[None, None]


def solution(mesh):
    in_specs = (P("depth", "rows"), P("depth", "rows"), P("rows", None, None), P(), P(), P())
    out_specs = P("rows", "depth", None, None)
    return jax.shard_map(body, mesh=mesh, in_specs=in_specs, out_specs=out_specs, check_vma=False)
```

```python
import jax
import jax.numpy as jnp
from jax import lax
from jax.experimental import pallas as pl
from jax.experimental.pallas import tpu as pltpu
from jax.sharding import PartitionSpec as P

PAIR_MOST = 2
SMEM = pl.BlockSpec(memory_space=pltpu.SMEM)
VMEM = pl.BlockSpec(memory_space=pltpu.VMEM)
PARAMS = pltpu.CompilerParams(vmem_limit_bytes=12 * 2**20)


def tile_cols(index, width):
    return pl.ds(pl.multiple_of(index * width, width), width)


def send_xg_kernel(
    own_ref, count_ref, col_ref, row_ref, x_ref, dy_ref, a_ref, out_ref, asked_ref, mine_ref, term_ref
):
    slots, width = a_ref.shape[0], a_ref.shape[1]
    peers, most = out_ref.shape[0], out_ref.shape[1] // 2
    row_tiles = x_ref.shape[1] // width
    own = own_ref[0]
    my_count = count_ref[own]
    owners = [col_ref[s, own] // row_tiles for s in range(slots)]
    places = []
    for s in range(slots):
        row = row_ref[s, own]
        rank = jnp.int32(0)
        for earlier in range(s):
            rank = rank + jnp.where(owners[earlier] == owners[s], 1, 0)
        place = jnp.where(s < my_count, owners[s] * most + rank, -1)
        places.append(place)
        mine_ref[s] = place
        mine_ref[slots + s] = row
        dy = dy_ref[:, tile_cols(row, width)]
        term_ref[s] = jnp.dot(dy, a_ref[s], preferred_element_type=jnp.float32).astype(out_ref.dtype)
    for r in range(peers):
        first, last = jnp.int32(0), jnp.int32(0)
        for s in range(slots):
            col = col_ref[s, r]
            code = jnp.where((col // row_tiles == own) & (s < count_ref[r]), col % row_tiles + 1, 0)
            last = jnp.where((first > 0) & (code > 0), code, last)
            first = jnp.where(first > 0, first, code)
        asked_ref[0, r] = first
        asked_ref[1, r] = last
        for k, code in enumerate((first, last)):
            out_ref[r, k] = x_ref[:, tile_cols(jnp.maximum(code - 1, 0), width)]
        for k in range(most):
            out_ref[r, most + k] = jnp.zeros(out_ref.shape[2:], out_ref.dtype)
    for s in range(slots):
        place = places[s]

        @pl.when(place >= 0)
        def _():
            out_ref[place // most, most + place % most] = term_ref[s]


def h_kernel(mine_ref, asked_ref, in_ref, a_ref, out_ref, acc_ref):
    slots = a_ref.shape[0]
    peers, most = out_ref.shape[0], out_ref.shape[1]
    row_tiles = acc_ref.shape[0]
    sums = [jnp.zeros(acc_ref.shape[1:], jnp.float32) for _ in range(row_tiles)]
    for s in range(slots):
        held = jnp.maximum(mine_ref[s], 0)
        row = mine_ref[slots + s]
        x = in_ref[held // most, held % most]
        term = lax.dot_general(x, a_ref[s], (((1,), (1,)), ((), ())), preferred_element_type=jnp.float32)
        for t in range(row_tiles):
            sums[t] = sums[t] + jnp.where((row == t) & (mine_ref[s] >= 0), term, 0.0)
    for t in range(row_tiles):
        acc_ref[t] = sums[t].astype(acc_ref.dtype)
    for r in range(peers):
        for k in range(most):
            out_ref[r, k] = acc_ref[jnp.maximum(asked_ref[k, r] - 1, 0)]


def fill_kernel(mine_ref, asked_ref, in_ref, dy_ref, z_ref, acc_ref):
    peers, most = in_ref.shape[0], in_ref.shape[1] // 2
    slots, row_tiles = z_ref.shape[0], acc_ref.shape[0]
    width = acc_ref.shape[2]
    sums = [jnp.zeros(acc_ref.shape[1:], jnp.float32) for _ in range(row_tiles)]
    for r in range(peers):
        for k in range(most):
            term = in_ref[r, most + k].astype(jnp.float32)
            code = asked_ref[k, r]
            for t in range(row_tiles):
                sums[t] = sums[t] + jnp.where(code == t + 1, term, 0.0)
    for t in range(row_tiles):
        acc_ref[t] = sums[t].astype(acc_ref.dtype)
    for s in range(slots):
        held = jnp.maximum(mine_ref[s], 0)
        row = mine_ref[slots + s]
        z_ref[s, 0] = dy_ref[:, tile_cols(row, width)]
        z_ref[s, 1] = acc_ref[row]
        z_ref[s, 2] = in_ref[held // most, held % most]


def join_kernel(mine_ref, in_ref, part_ref, z_ref):
    most = in_ref.shape[1]
    ready = part_ref.shape[1]
    for s in range(z_ref.shape[0]):
        held = jnp.maximum(mine_ref[s], 0)
        z_ref[s, :ready] = part_ref[s]
        z_ref[s, ready] = in_ref[held // most, held % most]


def exchange(value, axis):
    return lax.all_to_all(value, axis, 0, 0, tiled=True)


def near(value):
    return pltpu.with_memory_space_constraint(value, pltpu.VMEM)


def body(node_feat, grad_out, adjacency, tile_count, tile_row, tile_col):
    slots, width = adjacency.shape[0], adjacency.shape[1]
    feat = node_feat.shape[0]
    row_tiles = node_feat.shape[1] // width
    own_index = lax.axis_index("rows")
    peers = lax.axis_size("rows")
    bf16 = node_feat.dtype
    xg_type = jax.ShapeDtypeStruct((peers, 2 * PAIR_MOST, feat, width), bf16)
    h_type = jax.ShapeDtypeStruct((peers, PAIR_MOST, feat, width), bf16)
    asked_type = jax.ShapeDtypeStruct((PAIR_MOST, peers), jnp.int32)
    mine_type = jax.ShapeDtypeStruct((2 * slots,), jnp.int32)
    part_type = jax.ShapeDtypeStruct((slots, 3, feat, width), bf16)
    z_type = jax.ShapeDtypeStruct((slots, 4, feat, width), bf16)
    tiles = pltpu.VMEM((row_tiles, feat, width), bf16)
    adjacency = near(adjacency)

    xg_out, asked, mine = pl.pallas_call(
        send_xg_kernel,
        out_shape=(xg_type, asked_type, mine_type),
        in_specs=[SMEM, SMEM, SMEM, SMEM, VMEM, VMEM, VMEM],
        out_specs=(VMEM, SMEM, SMEM),
        compiler_params=PARAMS,
        scratch_shapes=[pltpu.VMEM((slots, feat, width), bf16)],
    )(own_index[None], tile_count, tile_col.T, tile_row.T, node_feat, grad_out, adjacency)
    xg_in = near(exchange(xg_out, "rows"))
    h_out = pl.pallas_call(
        h_kernel,
        out_shape=h_type,
        in_specs=[SMEM, SMEM, VMEM, VMEM],
        out_specs=VMEM,
        compiler_params=PARAMS,
        scratch_shapes=[tiles],
    )(mine, asked, xg_in, adjacency)
    h_in = near(exchange(h_out, "rows"))
    z_part = pl.pallas_call(
        fill_kernel,
        out_shape=part_type,
        in_specs=[SMEM, SMEM, VMEM, VMEM],
        out_specs=VMEM,
        compiler_params=PARAMS,
        scratch_shapes=[tiles],
    )(mine, asked, xg_in, grad_out)
    z_out = pl.pallas_call(
        join_kernel,
        out_shape=z_type,
        in_specs=[SMEM, VMEM, VMEM],
        out_specs=VMEM,
        compiler_params=PARAMS,
    )(mine, h_in, near(z_part))
    z_in = exchange(z_out, "depth")
    result = jnp.einsum("qfa,qfb->ab", z_in[:, 0], z_in[:, 3], preferred_element_type=jnp.float32)
    result += jnp.einsum("qfa,qfb->ab", z_in[:, 1], z_in[:, 2], preferred_element_type=jnp.float32)
    count = lax.dynamic_index_in_dim(tile_count, own_index, 0, keepdims=False)
    return jnp.where(lax.axis_index("depth") < count, result, 0.0)[None, None]


def solution(mesh):
    in_specs = (P("depth", "rows"), P("depth", "rows"), P("rows", None, None), P(), P(), P())
    out_specs = P("rows", "depth", None, None)
    return jax.shard_map(body, mesh=mesh, in_specs=in_specs, out_specs=out_specs, check_vma=False)
```

```python
import jax
import jax.numpy as jnp
from jax import lax
from jax.experimental import pallas as pl
from jax.experimental.pallas import tpu as pltpu
from jax.sharding import PartitionSpec as P

PAIR_MOST = 2
LOADS = 4
STORES = 4
SMEM = pl.BlockSpec(memory_space=pltpu.SMEM)
VMEM = pl.BlockSpec(memory_space=pltpu.VMEM)
ANY = pl.BlockSpec(memory_space=pl.ANY)
HBM = pl.BlockSpec(memory_space=pltpu.HBM)
PARAMS = pltpu.CompilerParams(vmem_limit_bytes=12 * 2**20)


def tile_cols(index, width):
    return pl.ds(pl.multiple_of(index * width, width), width)


def send_xg_kernel(
    own_ref, col_ref, row_ref, count_ref, cols_ref, counts_ref, x_ref, dy_ref, a_hbm,
    out_ref, asked_ref, mine_ref, a_ref, term_ref, code_ref, a_sem, code_sem,
):
    slots, width = a_ref.shape[0], a_ref.shape[1]
    peers, most = out_ref.shape[0], out_ref.shape[1] // 2
    row_tiles = x_ref.shape[1] // width
    loads = []
    for c in range(LOADS):
        part = pl.ds(c * (slots // LOADS), slots // LOADS)
        loads.append(pltpu.make_async_copy(a_hbm.at[part], a_ref.at[part], a_sem.at[c]))
        loads[c].start()
    own = own_ref[0]
    cols = cols_ref[...]
    slot_ids = lax.broadcasted_iota(jnp.int32, cols.shape, 0)
    wanted = (slot_ids < counts_ref[...]) & (cols // row_tiles == own)
    code = cols % row_tiles + 1
    first = jnp.max(jnp.where(wanted, (slots - 1 - slot_ids) * 8 + code, 0), axis=0, keepdims=True)
    last = jnp.max(jnp.where(wanted, slot_ids * 8 + code, 0), axis=0, keepdims=True)
    two = first // 8 + last // 8 != slots - 1
    code_ref[0:1] = first % 8
    code_ref[1:2] = jnp.where(two, last % 8, 0)
    to_scalars = pltpu.make_async_copy(code_ref, asked_ref, code_sem)
    to_scalars.start()
    owners = [col_ref[s, own] // row_tiles for s in range(slots)]
    places = []
    for s in range(slots):
        row = row_ref[s, own]
        rank = jnp.int32(0)
        for earlier in range(s):
            rank = rank + jnp.where(owners[earlier] == owners[s], 1, 0)
        place = jnp.where(s < count_ref[own], owners[s] * most + rank, -1)
        places.append(place)
        mine_ref[s] = place
        mine_ref[slots + s] = row
    to_scalars.wait()
    for r in range(peers):
        for k in range(most):
            t = jnp.maximum(asked_ref[k, r] - 1, 0)
            out_ref[r, k] = x_ref[:, tile_cols(t, width)]
            out_ref[r, most + k] = jnp.zeros(out_ref.shape[2:], out_ref.dtype)
    for s in range(slots):
        if s % (slots // LOADS) == 0:
            loads[s // (slots // LOADS)].wait()
        dy = dy_ref[:, tile_cols(mine_ref[slots + s], width)]
        term_ref[s] = jnp.dot(dy, a_ref[s], preferred_element_type=jnp.float32).astype(out_ref.dtype)
    for s in range(slots):
        place = places[s]

        @pl.when(place >= 0)
        def _():
            out_ref[place // most, most + place % most] = term_ref[s]


def h_kernel(mine_ref, asked_ref, in_ref, a_ref, out_hbm, acc_ref, out_ref, out_sem):
    slots = a_ref.shape[0]
    peers, most = out_ref.shape[0], out_ref.shape[1]
    row_tiles = acc_ref.shape[0]
    sums = [jnp.zeros(acc_ref.shape[1:], jnp.float32) for _ in range(row_tiles)]
    for s in range(slots):
        held = jnp.maximum(mine_ref[s], 0)
        row = mine_ref[slots + s]
        x = in_ref[held // most, held % most]
        term = lax.dot_general(x, a_ref[s], (((1,), (1,)), ((), ())), preferred_element_type=jnp.float32)
        for t in range(row_tiles):
            sums[t] = sums[t] + jnp.where((row == t) & (mine_ref[s] >= 0), term, 0.0)
    for t in range(row_tiles):
        acc_ref[t] = sums[t].astype(acc_ref.dtype)
    stores = []
    for r in range(peers):
        for k in range(most):
            out_ref[r, k] = acc_ref[jnp.maximum(asked_ref[k, r] - 1, 0)]
        if (r + 1) % (peers // STORES) == 0:
            part = pl.ds(r + 1 - peers // STORES, peers // STORES)
            copy = pltpu.make_async_copy(out_ref.at[part], out_hbm.at[part], out_sem.at[len(stores)])
            copy.start()
            stores.append(copy)
    for copy in stores:
        copy.wait()


def fill_kernel(mine_ref, asked_ref, in_ref, dy_ref, z_ref, acc_ref):
    peers, most = in_ref.shape[0], in_ref.shape[1] // 2
    slots, row_tiles = z_ref.shape[0], acc_ref.shape[0]
    width = acc_ref.shape[2]
    sums = [jnp.zeros(acc_ref.shape[1:], jnp.float32) for _ in range(row_tiles)]
    for r in range(peers):
        for k in range(most):
            term = in_ref[r, most + k].astype(jnp.float32)
            code = asked_ref[k, r]
            for t in range(row_tiles):
                sums[t] = sums[t] + jnp.where(code == t + 1, term, 0.0)
    for t in range(row_tiles):
        acc_ref[t] = sums[t].astype(acc_ref.dtype)
    for s in range(slots):
        held = jnp.maximum(mine_ref[s], 0)
        row = mine_ref[slots + s]
        z_ref[s, 0] = dy_ref[:, tile_cols(row, width)]
        z_ref[s, 1] = acc_ref[row]
        z_ref[s, 2] = in_ref[held // most, held % most]


def join_kernel(mine_ref, in_ref, part_ref, z_ref, sem):
    del part_ref
    most = in_ref.shape[1]
    copies = []
    for s in range(z_ref.shape[0]):
        held = jnp.maximum(mine_ref[s], 0)
        copies.append(pltpu.make_async_copy(in_ref.at[held // most, held % most], z_ref.at[s, 3], sem.at[s]))
        copies[s].start()
    for copy in copies:
        copy.wait()


def exchange(value, axis):
    return lax.all_to_all(value, axis, 0, 0, tiled=True)


def far(value):
    return pltpu.with_memory_space_constraint(value, pltpu.HBM)


def near(value):
    return pltpu.with_memory_space_constraint(value, pltpu.VMEM)


def body(node_feat, grad_out, adjacency, tile_count, tile_row, tile_col):
    slots, width = adjacency.shape[0], adjacency.shape[1]
    feat = node_feat.shape[0]
    row_tiles = node_feat.shape[1] // width
    own_index = lax.axis_index("rows")
    peers = lax.axis_size("rows")
    bf16 = node_feat.dtype
    xg_type = jax.ShapeDtypeStruct((peers, 2 * PAIR_MOST, feat, width), bf16)
    h_type = jax.ShapeDtypeStruct((peers, PAIR_MOST, feat, width), bf16)
    asked_type = jax.ShapeDtypeStruct((PAIR_MOST, peers), jnp.int32)
    mine_type = jax.ShapeDtypeStruct((2 * slots,), jnp.int32)
    z_type = jax.ShapeDtypeStruct((slots, 4, feat, width), bf16)
    tiles = pltpu.VMEM((row_tiles, feat, width), bf16)
    node_feat, grad_out, adjacency = far(node_feat), far(grad_out), far(adjacency)
    cols, counts = tile_col.T, tile_count

    xg_out, asked, mine = pl.pallas_call(
        send_xg_kernel,
        out_shape=(xg_type, asked_type, mine_type),
        in_specs=[SMEM, SMEM, SMEM, SMEM, VMEM, VMEM, VMEM, VMEM, ANY],
        out_specs=(VMEM, SMEM, SMEM),
        compiler_params=PARAMS,
        scratch_shapes=[
            pltpu.VMEM(adjacency.shape, bf16),
            pltpu.VMEM((slots, feat, width), bf16),
            pltpu.VMEM(asked_type.shape, jnp.int32),
            pltpu.SemaphoreType.DMA((LOADS,)),
            pltpu.SemaphoreType.DMA,
        ],
    )(
        own_index[None], far(cols), far(tile_row.T), far(counts), far(cols), far(counts[None]),
        node_feat, grad_out, adjacency,
    )
    xg_in = near(exchange(xg_out, "rows"))
    h_out = pl.pallas_call(
        h_kernel,
        out_shape=h_type,
        in_specs=[SMEM, SMEM, VMEM, VMEM],
        out_specs=HBM,
        compiler_params=PARAMS,
        scratch_shapes=[tiles, pltpu.VMEM(h_type.shape, bf16), pltpu.SemaphoreType.DMA((STORES,))],
    )(mine, asked, xg_in, near(adjacency))
    h_in = near(exchange(h_out, "rows"))
    z_part = pl.pallas_call(
        fill_kernel,
        out_shape=z_type,
        in_specs=[SMEM, SMEM, VMEM, VMEM],
        out_specs=VMEM,
        compiler_params=PARAMS,
        scratch_shapes=[tiles],
    )(mine, asked, xg_in, grad_out)
    z_out = pl.pallas_call(
        join_kernel,
        out_shape=z_type,
        in_specs=[SMEM, VMEM, HBM],
        out_specs=HBM,
        compiler_params=PARAMS,
        input_output_aliases={2: 0},
        scratch_shapes=[pltpu.SemaphoreType.DMA((slots,))],
    )(mine, h_in, z_part)
    z_in = exchange(z_out, "depth")
    result = jnp.einsum("qfa,qfb->ab", z_in[:, 0], z_in[:, 3], preferred_element_type=jnp.float32)
    result += jnp.einsum("qfa,qfb->ab", z_in[:, 1], z_in[:, 2], preferred_element_type=jnp.float32)
    count = lax.dynamic_index_in_dim(tile_count, own_index, 0, keepdims=False)
    return jnp.where(lax.axis_index("depth") < count, result, 0.0)[None, None]


def solution(mesh):
    in_specs = (P("depth", "rows"), P("depth", "rows"), P("rows", None, None), P(), P(), P())
    out_specs = P("rows", "depth", None, None)
    return jax.shard_map(body, mesh=mesh, in_specs=in_specs, out_specs=out_specs, check_vma=False)
```

```python
import jax
import jax.numpy as jnp
from jax import lax
from jax.experimental import pallas as pl
from jax.experimental.pallas import tpu as pltpu
from jax.sharding import PartitionSpec as P

PAIR_MOST = 2
LOADS = 4
STORES = 4
LANES = 128
SMEM = pl.BlockSpec(memory_space=pltpu.SMEM)
VMEM = pl.BlockSpec(memory_space=pltpu.VMEM)
ANY = pl.BlockSpec(memory_space=pl.ANY)
HBM = pl.BlockSpec(memory_space=pltpu.HBM)
PARAMS = pltpu.CompilerParams(vmem_limit_bytes=12 * 2**20)


def tile_cols(index, width):
    return pl.ds(pl.multiple_of(index * width, width), width)


def send_xg_kernel(
    own_ref, col_ref, row_ref, count_ref, cols_ref, counts_ref, x_ref, dy_ref, a_hbm,
    out_ref, asked_ref, mine_ref, spare_ref, a_ref, term_ref, code_ref, a_sem, code_sem,
):
    del spare_ref
    slots, width = a_ref.shape[0], a_ref.shape[1]
    peers, most = out_ref.shape[0], PAIR_MOST
    feat = x_ref.shape[0]
    row_tiles = x_ref.shape[1] // width
    loads = []
    for c in range(LOADS):
        part = pl.ds(c * (slots // LOADS), slots // LOADS)
        loads.append(pltpu.make_async_copy(a_hbm.at[part], a_ref.at[part], a_sem.at[c]))
        loads[c].start()
    own = own_ref[0]
    cols = cols_ref[...]
    slot_ids = lax.broadcasted_iota(jnp.int32, cols.shape, 0)
    wanted = (slot_ids < counts_ref[...]) & (cols // row_tiles == own)
    code = cols % row_tiles + 1
    first = jnp.max(jnp.where(wanted, (slots - 1 - slot_ids) * 8 + code, 0), axis=0, keepdims=True)
    last = jnp.max(jnp.where(wanted, slot_ids * 8 + code, 0), axis=0, keepdims=True)
    two = first // 8 + last // 8 != slots - 1
    code_ref[0:1] = first % 8
    code_ref[1:2] = jnp.where(two, last % 8, 0)
    to_scalars = pltpu.make_async_copy(code_ref, asked_ref, code_sem)
    to_scalars.start()
    owners = [col_ref[s, own] // row_tiles for s in range(slots)]
    for s in range(slots):
        row = row_ref[s, own]
        rank = jnp.int32(0)
        for earlier in range(s):
            rank = rank + jnp.where(owners[earlier] == owners[s], 1, 0)
        mine_ref[s] = jnp.where(s < count_ref[own], owners[s] * most + rank, -1)
        mine_ref[slots + s] = row
    to_scalars.wait()
    for r in range(peers):
        for k in range(most):
            t = jnp.maximum(asked_ref[k, r] - 1, 0)
            out_ref[r, k * feat : (k + 1) * feat] = x_ref[:, tile_cols(t, width)]
    for s in range(slots):
        if s % (slots // LOADS) == 0:
            loads[s // (slots // LOADS)].wait()
        dy = dy_ref[:, tile_cols(mine_ref[slots + s], width)]
        term = jnp.dot(dy, a_ref[s], preferred_element_type=jnp.float32)
        for lanes, half in enumerate(term_ref):
            half[s * feat : (s + 1) * feat] = term[:, lanes * LANES : (lanes + 1) * LANES]
    for r in range(peers):
        for lanes, half in enumerate(term_ref):
            of_feature = half[pl.ds(r, slots, stride=feat)].astype(out_ref.dtype)
            out_ref[r, most * feat :, lanes * LANES : (lanes + 1) * LANES] = of_feature


def h_kernel(
    mine_ref, asked_ref, cols_ref, counts_ref, in_ref, a_ref, spare_ref,
    out_hbm, acc_ref, pick_ref, sum_ref, out_ref, out_sem,
):
    del spare_ref
    slots = a_ref.shape[0]
    peers, most = out_ref.shape[0], PAIR_MOST
    row_tiles, feat, width = acc_ref.shape
    sums = [jnp.zeros((feat, width), jnp.float32) for _ in range(row_tiles)]
    for s in range(slots):
        held = jnp.maximum(mine_ref[s], 0)
        row = mine_ref[slots + s]
        x = in_ref[held // most, pl.ds(pl.multiple_of(held % most * feat, feat), feat)]
        term = lax.dot_general(x, a_ref[s], (((1,), (1,)), ((), ())), preferred_element_type=jnp.float32)
        for t in range(row_tiles):
            sums[t] = sums[t] + jnp.where((row == t) & (mine_ref[s] >= 0), term, 0.0)
    for t in range(row_tiles):
        acc_ref[t] = sums[t].astype(acc_ref.dtype)
    cols = cols_ref[...]
    live = lax.broadcasted_iota(jnp.int32, cols.shape, 0) < counts_ref[...]
    cols = jnp.where(live, cols, -1)
    tile_ids = lax.broadcasted_iota(jnp.int32, (slots, peers * row_tiles), 1)
    for r in range(peers):
        pick_ref[r * slots : (r + 1) * slots] = (cols[:, r : r + 1] == tile_ids).astype(pick_ref.dtype)
    terms = in_ref[:, most * feat :].reshape(peers * slots, width)
    sum_ref[: peers * row_tiles] = lax.dot_general(
        pick_ref[...], terms, (((0,), (0,)), ((), ())), preferred_element_type=jnp.float32
    )
    sum_ref[peers * row_tiles :] = jnp.zeros((row_tiles, width), jnp.float32)
    stores = []
    for r in range(peers):
        for k in range(most):
            out_ref[r, k * feat : (k + 1) * feat] = acc_ref[jnp.maximum(asked_ref[k, r] - 1, 0)]
        of_tiles = sum_ref[r * row_tiles : (r + 2) * row_tiles]
        out_ref[r, most * feat :] = of_tiles.astype(out_ref.dtype)
        if (r + 1) % (peers // STORES) == 0:
            part = pl.ds(r + 1 - peers // STORES, peers // STORES)
            copy = pltpu.make_async_copy(out_ref.at[part], out_hbm.at[part], out_sem.at[len(stores)])
            copy.start()
            stores.append(copy)
    for copy in stores:
        copy.wait()


def fill_kernel(mine_ref, in_ref, dy_ref, z_ref):
    slots, _, feat, width = z_ref.shape
    for s in range(slots):
        held = jnp.maximum(mine_ref[s], 0)
        z_ref[s, 0] = dy_ref[:, tile_cols(mine_ref[slots + s], width)]
        z_ref[s, 2] = in_ref[held // PAIR_MOST, pl.ds(pl.multiple_of(held % PAIR_MOST * feat, feat), feat)]


def join_kernel(mine_ref, in_ref, part_ref, z_ref, rows_ref, g_ref, sem):
    del part_ref
    peers, most = in_ref.shape[0], PAIR_MOST
    slots = z_ref.shape[0]
    row_tiles, feat, _ = g_ref.shape
    copies = []
    for s in range(slots):
        held = jnp.maximum(mine_ref[s], 0)
        tile = in_ref.at[held // most, pl.ds(pl.multiple_of(held % most * feat, feat), feat)]
        copies.append(pltpu.make_async_copy(tile, z_ref.at[s, 3], sem.at[s]))
        copies[s].start()
    step = in_ref.shape[1] - most * feat
    for r in range(peers):
        of_tiles = in_ref[r, most * feat :].astype(jnp.float32)
        for lanes, half in enumerate(rows_ref):
            half[r * step : (r + 1) * step] = of_tiles[:, lanes * LANES : (lanes + 1) * LANES]
    for t in range(row_tiles):
        for lanes, half in enumerate(rows_ref):
            of_tile = half[pl.ds(t, feat, stride=step)].astype(g_ref.dtype)
            g_ref[t, :, lanes * LANES : (lanes + 1) * LANES] = of_tile
    for s in range(slots):
        copies.append(pltpu.make_async_copy(g_ref.at[mine_ref[slots + s]], z_ref.at[s, 1], sem.at[slots + s]))
        copies[slots + s].start()
    for copy in copies:
        copy.wait()


def exchange(value, axis):
    return lax.all_to_all(value, axis, 0, 0, tiled=True)


def far(value):
    return pltpu.with_memory_space_constraint(value, pltpu.HBM)


def near(value):
    return pltpu.with_memory_space_constraint(value, pltpu.VMEM)


def body(node_feat, grad_out, adjacency, tile_count, tile_row, tile_col):
    slots, width = adjacency.shape[0], adjacency.shape[1]
    feat = node_feat.shape[0]
    row_tiles = node_feat.shape[1] // width
    own_index = lax.axis_index("rows")
    peers = lax.axis_size("rows")
    bf16 = node_feat.dtype
    wanted_rows = PAIR_MOST * feat
    xg_type = jax.ShapeDtypeStruct((peers, wanted_rows + slots, width), bf16)
    hg_type = jax.ShapeDtypeStruct((peers, wanted_rows + 2 * row_tiles, width), bf16)
    asked_type = jax.ShapeDtypeStruct((PAIR_MOST, peers), jnp.int32)
    mine_type = jax.ShapeDtypeStruct((2 * slots,), jnp.int32)
    z_type = jax.ShapeDtypeStruct((slots, 4, feat, width), bf16)
    tiles = pltpu.VMEM((row_tiles, feat, width), bf16)
    node_feat, grad_out, adjacency = far(node_feat), far(grad_out), far(adjacency)
    cols, counts = tile_col.T, tile_count[None]

    xg_out, asked, mine, spare = pl.pallas_call(
        send_xg_kernel,
        out_shape=(xg_type, asked_type, mine_type, hg_type),
        in_specs=[SMEM, SMEM, SMEM, SMEM, VMEM, VMEM, VMEM, VMEM, ANY],
        out_specs=(VMEM, SMEM, SMEM, HBM),
        compiler_params=PARAMS,
        scratch_shapes=[
            pltpu.VMEM(adjacency.shape, bf16),
            [pltpu.VMEM((slots * feat, LANES), jnp.float32)] * (width // LANES),
            pltpu.VMEM(asked_type.shape, jnp.int32),
            pltpu.SemaphoreType.DMA((LOADS,)),
            pltpu.SemaphoreType.DMA,
        ],
    )(
        own_index[None], far(cols), far(tile_row.T), far(tile_count), far(cols), far(counts),
        node_feat, grad_out, adjacency,
    )
    xg_in = near(exchange(xg_out, "rows"))
    hg_out = pl.pallas_call(
        h_kernel,
        out_shape=hg_type,
        in_specs=[SMEM, SMEM, VMEM, VMEM, VMEM, VMEM, HBM],
        out_specs=HBM,
        input_output_aliases={6: 0},
        compiler_params=PARAMS,
        scratch_shapes=[
            tiles,
            pltpu.VMEM((peers * slots, peers * row_tiles), bf16),
            pltpu.VMEM(((peers + 1) * row_tiles, width), jnp.float32),
            pltpu.VMEM(hg_type.shape, bf16),
            pltpu.SemaphoreType.DMA((STORES,)),
        ],
    )(mine, asked, near(cols), near(counts), xg_in, near(adjacency), far(spare))
    hg_in = near(exchange(hg_out, "rows"))
    z_part = pl.pallas_call(
        fill_kernel,
        out_shape=z_type,
        in_specs=[SMEM, VMEM, VMEM],
        out_specs=VMEM,
        compiler_params=PARAMS,
    )(mine, xg_in, grad_out)
    z_out = pl.pallas_call(
        join_kernel,
        out_shape=z_type,
        in_specs=[SMEM, VMEM, HBM],
        out_specs=HBM,
        compiler_params=PARAMS,
        input_output_aliases={2: 0},
        scratch_shapes=[
            [pltpu.VMEM((peers * 2 * row_tiles, LANES), jnp.float32)] * (width // LANES),
            tiles,
            pltpu.SemaphoreType.DMA((2 * slots,)),
        ],
    )(mine, hg_in, z_part)
    z_in = exchange(z_out, "depth")
    result = jnp.einsum("qfa,qfb->ab", z_in[:, 0], z_in[:, 3], preferred_element_type=jnp.float32)
    result += jnp.einsum("qfa,qfb->ab", z_in[:, 1], z_in[:, 2], preferred_element_type=jnp.float32)
    count = lax.dynamic_index_in_dim(tile_count, own_index, 0, keepdims=False)
    return jnp.where(lax.axis_index("depth") < count, result, 0.0)[None, None]


def solution(mesh):
    in_specs = (P("depth", "rows"), P("depth", "rows"), P("rows", None, None), P(), P(), P())
    out_specs = P("rows", "depth", None, None)
    return jax.shard_map(body, mesh=mesh, in_specs=in_specs, out_specs=out_specs, check_vma=False)
```

```python
import jax
import jax.numpy as jnp
from jax import lax
from jax.experimental import pallas as pl
from jax.experimental.pallas import tpu as pltpu
from jax.sharding import PartitionSpec as P

PAIR_MOST = 2
LOADS = 4
STORES = 4
LANES = 128
GROUP = 4
SMEM = pl.BlockSpec(memory_space=pltpu.SMEM)
VMEM = pl.BlockSpec(memory_space=pltpu.VMEM)
ANY = pl.BlockSpec(memory_space=pl.ANY)
HBM = pl.BlockSpec(memory_space=pltpu.HBM)
PARAMS = pltpu.CompilerParams(vmem_limit_bytes=12 * 2**20)


def tile_cols(index, width):
    return pl.ds(pl.multiple_of(index * width, width), width)


def send_xg_kernel(
    own_ref, col_ref, row_ref, count_ref, cols_ref, counts_ref, x_ref, dy_ref, a_hbm,
    out_ref, asked_ref, mine_ref, dy0_ref, dy1_ref, dy2_ref, dy3_ref, a_ref, term_ref, code_ref, a_sem, code_sem,
):
    slots, width = a_ref.shape[0], a_ref.shape[1]
    peers, most = out_ref.shape[0], PAIR_MOST
    feat = x_ref.shape[0]
    row_tiles = x_ref.shape[1] // width
    loads = []
    for c in range(LOADS):
        part = pl.ds(c * (slots // LOADS), slots // LOADS)
        loads.append(pltpu.make_async_copy(a_hbm.at[part], a_ref.at[part], a_sem.at[c]))
        loads[c].start()
    own = own_ref[0]
    cols = cols_ref[...]
    slot_ids = lax.broadcasted_iota(jnp.int32, cols.shape, 0)
    wanted = (slot_ids < counts_ref[...]) & (cols // row_tiles == own)
    code = cols % row_tiles + 1
    first = jnp.max(jnp.where(wanted, (slots - 1 - slot_ids) * 8 + code, 0), axis=0, keepdims=True)
    last = jnp.max(jnp.where(wanted, slot_ids * 8 + code, 0), axis=0, keepdims=True)
    two = first // 8 + last // 8 != slots - 1
    code_ref[0:1] = first % 8
    code_ref[1:2] = jnp.where(two, last % 8, 0)
    to_scalars = pltpu.make_async_copy(code_ref, asked_ref, code_sem)
    to_scalars.start()
    owners = [col_ref[s, own] // row_tiles for s in range(slots)]
    for s in range(slots):
        row = row_ref[s, own]
        rank = jnp.int32(0)
        for earlier in range(s):
            rank = rank + jnp.where(owners[earlier] == owners[s], 1, 0)
        mine_ref[s] = jnp.where(s < count_ref[own], owners[s] * most + rank, -1)
        mine_ref[slots + s] = row
    for step, part_ref in enumerate((dy0_ref, dy1_ref, dy2_ref, dy3_ref)):
        group = own_ref[1] // GROUP ^ step
        for e in range(GROUP):
            part_ref[e] = dy_ref[:, tile_cols(row_ref[group * GROUP + e, own], width)]
    to_scalars.wait()
    for r in range(peers):
        for k in range(most):
            t = jnp.maximum(asked_ref[k, r] - 1, 0)
            out_ref[r, k * feat : (k + 1) * feat] = x_ref[:, tile_cols(t, width)]
    for s in range(slots):
        if s % (slots // LOADS) == 0:
            loads[s // (slots // LOADS)].wait()
        dy = dy_ref[:, tile_cols(mine_ref[slots + s], width)]
        term = jnp.dot(dy, a_ref[s], preferred_element_type=jnp.float32)
        for lanes, half in enumerate(term_ref):
            half[s * feat : (s + 1) * feat] = term[:, lanes * LANES : (lanes + 1) * LANES]
    for r in range(peers):
        for lanes, half in enumerate(term_ref):
            of_feature = half[pl.ds(r, slots, stride=feat)].astype(out_ref.dtype)
            out_ref[r, most * feat :, lanes * LANES : (lanes + 1) * LANES] = of_feature


def h_kernel(
    mine_ref, asked_ref, cols_ref, counts_ref, in_ref, a_ref,
    out_hbm, acc_ref, pick_ref, sum_ref, out_ref, out_sem,
):
    slots = a_ref.shape[0]
    peers, most = out_ref.shape[0], PAIR_MOST
    row_tiles, feat, width = acc_ref.shape
    sums = [jnp.zeros((feat, width), jnp.float32) for _ in range(row_tiles)]
    for s in range(slots):
        held = jnp.maximum(mine_ref[s], 0)
        row = mine_ref[slots + s]
        x = in_ref[held // most, pl.ds(pl.multiple_of(held % most * feat, feat), feat)]
        term = lax.dot_general(x, a_ref[s], (((1,), (1,)), ((), ())), preferred_element_type=jnp.float32)
        for t in range(row_tiles):
            sums[t] = sums[t] + jnp.where((row == t) & (mine_ref[s] >= 0), term, 0.0)
    for t in range(row_tiles):
        acc_ref[t] = sums[t].astype(acc_ref.dtype)
    cols = cols_ref[...]
    live = lax.broadcasted_iota(jnp.int32, cols.shape, 0) < counts_ref[...]
    cols = jnp.where(live, cols, -1)
    tile_ids = lax.broadcasted_iota(jnp.int32, (slots, peers * row_tiles), 1)
    for r in range(peers):
        pick_ref[r * slots : (r + 1) * slots] = (cols[:, r : r + 1] == tile_ids).astype(pick_ref.dtype)
    terms = in_ref[:, most * feat :].reshape(peers * slots, width)
    sum_ref[: peers * row_tiles] = lax.dot_general(
        pick_ref[...], terms, (((0,), (0,)), ((), ())), preferred_element_type=jnp.float32
    )
    sum_ref[peers * row_tiles :] = jnp.zeros((row_tiles, width), jnp.float32)
    stores = []
    for r in range(peers):
        for k in range(most):
            out_ref[r, k * feat : (k + 1) * feat] = acc_ref[jnp.maximum(asked_ref[k, r] - 1, 0)]
        of_tiles = sum_ref[r * row_tiles : (r + 2) * row_tiles]
        out_ref[r, most * feat :] = of_tiles.astype(out_ref.dtype)
        if (r + 1) % (peers // STORES) == 0:
            part = pl.ds(r + 1 - peers // STORES, peers // STORES)
            copy = pltpu.make_async_copy(out_ref.at[part], out_hbm.at[part], out_sem.at[len(stores)])
            copy.start()
            stores.append(copy)
    for copy in stores:
        copy.wait()


def turn_kernel(own_ref, in0_ref, in1_ref, in2_ref, in3_ref, out0_ref, out1_ref, out2_ref, out3_ref):
    for e, out_ref in enumerate((out0_ref, out1_ref, out2_ref, out3_ref)):
        for g, in_ref in enumerate((in0_ref, in1_ref, in2_ref, in3_ref)):
            out_ref[g] = in_ref[own_ref[1] % GROUP ^ e]


def order_kernel(own_ref, in0_ref, in1_ref, in2_ref, in3_ref, out_ref):
    for e, in_ref in enumerate((in0_ref, in1_ref, in2_ref, in3_ref)):
        for g in range(GROUP):
            out_ref[own_ref[1] ^ (g * GROUP + e)] = in_ref[g]


def fill_kernel(mine_ref, in_ref, z_ref):
    slots, _, feat, _ = z_ref.shape
    for s in range(slots):
        held = jnp.maximum(mine_ref[s], 0)
        z_ref[s, 1] = in_ref[held // PAIR_MOST, pl.ds(pl.multiple_of(held % PAIR_MOST * feat, feat), feat)]


def join_kernel(mine_ref, in_ref, part_ref, z_ref, rows_ref, g_ref, sem):
    del part_ref
    peers, most = in_ref.shape[0], PAIR_MOST
    slots = z_ref.shape[0]
    row_tiles, feat, _ = g_ref.shape
    copies = []
    for s in range(slots):
        held = jnp.maximum(mine_ref[s], 0)
        tile = in_ref.at[held // most, pl.ds(pl.multiple_of(held % most * feat, feat), feat)]
        copies.append(pltpu.make_async_copy(tile, z_ref.at[s, 2], sem.at[s]))
        copies[s].start()
    step = in_ref.shape[1] - most * feat
    for r in range(peers):
        of_tiles = in_ref[r, most * feat :].astype(jnp.float32)
        for lanes, half in enumerate(rows_ref):
            half[r * step : (r + 1) * step] = of_tiles[:, lanes * LANES : (lanes + 1) * LANES]
    for t in range(row_tiles):
        for lanes, half in enumerate(rows_ref):
            of_tile = half[pl.ds(t, feat, stride=step)].astype(g_ref.dtype)
            g_ref[t, :, lanes * LANES : (lanes + 1) * LANES] = of_tile
    for s in range(slots):
        copies.append(pltpu.make_async_copy(g_ref.at[mine_ref[slots + s]], z_ref.at[s, 0], sem.at[slots + s]))
        copies[slots + s].start()
    for copy in copies:
        copy.wait()


def exchange(value, axis):
    return lax.all_to_all(value, axis, 0, 0, tiled=True)


def swap(value, step):
    if step == 0:
        return value
    places = range(lax.axis_size("depth"))
    return lax.ppermute(value, "depth", [(place, place ^ step) for place in places])


def hbm(kind):
    return pltpu.HBM(kind.shape, kind.dtype)


def far(value):
    return pltpu.with_memory_space_constraint(value, pltpu.HBM)


def near(value):
    return pltpu.with_memory_space_constraint(value, pltpu.VMEM)


def body(node_feat, grad_out, adjacency, tile_count, tile_row, tile_col):
    slots, width = adjacency.shape[0], adjacency.shape[1]
    feat = node_feat.shape[0]
    row_tiles = node_feat.shape[1] // width
    own_index = lax.axis_index("rows")
    peers = lax.axis_size("rows")
    bf16 = node_feat.dtype
    wanted_rows = PAIR_MOST * feat
    xg_type = jax.ShapeDtypeStruct((peers, wanted_rows + slots, width), bf16)
    hg_type = jax.ShapeDtypeStruct((peers, wanted_rows + 2 * row_tiles, width), bf16)
    asked_type = jax.ShapeDtypeStruct((PAIR_MOST, peers), jnp.int32)
    mine_type = jax.ShapeDtypeStruct((2 * slots,), jnp.int32)
    z_type = jax.ShapeDtypeStruct((slots, 3, feat, width), bf16)
    tiles = pltpu.VMEM((row_tiles, feat, width), bf16)
    slot_type = jax.ShapeDtypeStruct((slots, feat, width), bf16)
    node_feat, grad_out, adjacency = far(node_feat), far(grad_out), far(adjacency)
    cols, counts = tile_col.T, tile_count[None]

    four_type = jax.ShapeDtypeStruct((GROUP, feat, width), bf16)
    own = jnp.stack([own_index, lax.axis_index("depth")])
    xg_out, asked, mine, *dy_parts = pl.pallas_call(
        send_xg_kernel,
        out_shape=(hbm(xg_type), hbm(asked_type), hbm(mine_type)) + (hbm(four_type),) * GROUP,
        in_specs=[SMEM, SMEM, SMEM, SMEM, VMEM, VMEM, VMEM, VMEM, ANY],
        out_specs=(VMEM, SMEM, SMEM) + (VMEM,) * GROUP,
        compiler_params=PARAMS,
        scratch_shapes=[
            pltpu.VMEM(adjacency.shape, bf16),
            [pltpu.VMEM((slots * feat, LANES), jnp.float32)] * (width // LANES),
            pltpu.VMEM(asked_type.shape, jnp.int32),
            pltpu.SemaphoreType.DMA((LOADS,)),
            pltpu.SemaphoreType.DMA,
        ],
    )(
        own, far(cols), far(tile_row.T), far(tile_count), far(cols), far(counts),
        node_feat, grad_out, adjacency,
    )
    xg_in = exchange(xg_out, "rows")
    dy_parts = [swap(part, GROUP * step) for step, part in enumerate(dy_parts)]
    xg_in, *dy_parts = lax.optimization_barrier((xg_in, *dy_parts))
    hg_out = pl.pallas_call(
        h_kernel,
        out_shape=hbm(hg_type),
        in_specs=[SMEM, SMEM, VMEM, VMEM, VMEM, VMEM],
        out_specs=HBM,
        compiler_params=PARAMS,
        scratch_shapes=[
            tiles,
            pltpu.VMEM((peers * slots, peers * row_tiles), bf16),
            pltpu.VMEM(((peers + 1) * row_tiles, width), jnp.float32),
            pltpu.VMEM(hg_type.shape, bf16),
            pltpu.SemaphoreType.DMA((STORES,)),
        ],
    )(far(mine), far(asked), near(cols), near(counts), near(xg_in), near(adjacency))
    hg_in = exchange(hg_out, "rows")
    dy_parts = pl.pallas_call(
        turn_kernel,
        out_shape=(hbm(four_type),) * GROUP,
        in_specs=[SMEM] + [VMEM] * GROUP,
        out_specs=(VMEM,) * GROUP,
        compiler_params=PARAMS,
    )(own, *dy_parts)
    dy_parts = [swap(part, step) for step, part in enumerate(dy_parts)]
    hg_in, *dy_parts = lax.optimization_barrier((hg_in, *dy_parts))
    dy = pl.pallas_call(
        order_kernel,
        out_shape=slot_type,
        in_specs=[SMEM] + [VMEM] * GROUP,
        out_specs=VMEM,
        compiler_params=PARAMS,
    )(own, *dy_parts)
    z_part = pl.pallas_call(
        fill_kernel,
        out_shape=z_type,
        in_specs=[SMEM, VMEM],
        out_specs=VMEM,
        compiler_params=PARAMS,
    )(mine, near(xg_in))
    z_out = pl.pallas_call(
        join_kernel,
        out_shape=z_type,
        in_specs=[SMEM, VMEM, HBM],
        out_specs=HBM,
        compiler_params=PARAMS,
        input_output_aliases={2: 0},
        scratch_shapes=[
            [pltpu.VMEM((peers * 2 * row_tiles, LANES), jnp.float32)] * (width // LANES),
            tiles,
            pltpu.SemaphoreType.DMA((2 * slots,)),
        ],
    )(mine, near(hg_in), z_part)
    z_in = exchange(z_out, "depth")
    result = jnp.einsum("qfa,qfb->ab", dy, z_in[:, 2], preferred_element_type=jnp.float32)
    result += jnp.einsum("qfa,qfb->ab", z_in[:, 0], z_in[:, 1], preferred_element_type=jnp.float32)
    count = lax.dynamic_index_in_dim(tile_count, own_index, 0, keepdims=False)
    return jnp.where(lax.axis_index("depth") < count, result, 0.0)[None, None]


def solution(mesh):
    in_specs = (P("depth", "rows"), P("depth", "rows"), P("rows", None, None), P(), P(), P())
    out_specs = P("rows", "depth", None, None)
    return jax.shard_map(body, mesh=mesh, in_specs=in_specs, out_specs=out_specs, check_vma=False)
```

```python
import jax
import jax.numpy as jnp
from jax import lax
from jax.experimental import pallas as pl
from jax.experimental.pallas import tpu as pltpu
from jax.sharding import PartitionSpec as P

PAIR_MOST = 2
LOADS = 4
STORES = 4
LANES = 128
GROUP = 4
SMEM = pl.BlockSpec(memory_space=pltpu.SMEM)
VMEM = pl.BlockSpec(memory_space=pltpu.VMEM)
ANY = pl.BlockSpec(memory_space=pl.ANY)
HBM = pl.BlockSpec(memory_space=pltpu.HBM)
PARAMS = pltpu.CompilerParams(vmem_limit_bytes=12 * 2**20)


def tile_cols(index, width):
    return pl.ds(pl.multiple_of(index * width, width), width)


def send_xg_kernel(
    own_ref, col_ref, row_ref, count_ref, cols_ref, counts_ref, x_ref, dy_ref, a_hbm,
    out_ref, asked_ref, mine_ref, dy0_ref, dy1_ref, dy2_ref, dy3_ref, a_ref, term_ref, code_ref, a_sem, code_sem,
):
    slots, width = a_ref.shape[0], a_ref.shape[1]
    peers, most = out_ref.shape[0], PAIR_MOST
    feat = x_ref.shape[0]
    row_tiles = x_ref.shape[1] // width
    loads = []
    for c in range(LOADS):
        part = pl.ds(c * (slots // LOADS), slots // LOADS)
        loads.append(pltpu.make_async_copy(a_hbm.at[part], a_ref.at[part], a_sem.at[c]))
        loads[c].start()
    own = own_ref[0]
    cols = cols_ref[...]
    slot_ids = lax.broadcasted_iota(jnp.int32, cols.shape, 0)
    wanted = (slot_ids < counts_ref[...]) & (cols // row_tiles == own)
    code = cols % row_tiles + 1
    first = jnp.max(jnp.where(wanted, (slots - 1 - slot_ids) * 8 + code, 0), axis=0, keepdims=True)
    last = jnp.max(jnp.where(wanted, slot_ids * 8 + code, 0), axis=0, keepdims=True)
    two = first // 8 + last // 8 != slots - 1
    code_ref[0:1] = first % 8
    code_ref[1:2] = jnp.where(two, last % 8, 0)
    to_scalars = pltpu.make_async_copy(code_ref, asked_ref, code_sem)
    to_scalars.start()
    owners = [col_ref[s, own] // row_tiles for s in range(slots)]
    for s in range(slots):
        row = row_ref[s, own]
        rank = jnp.int32(0)
        for earlier in range(s):
            rank = rank + jnp.where(owners[earlier] == owners[s], 1, 0)
        mine_ref[s] = jnp.where(s < count_ref[own], owners[s] * most + rank, -1)
        mine_ref[slots + s] = row
    for step, part_ref in enumerate((dy0_ref, dy1_ref, dy2_ref, dy3_ref)):
        group = own_ref[1] // GROUP ^ step
        for e in range(GROUP):
            part_ref[e] = dy_ref[:, tile_cols(row_ref[group * GROUP + e, own], width)]
    to_scalars.wait()
    for r in range(peers):
        for k in range(most):
            t = jnp.maximum(asked_ref[k, r] - 1, 0)
            out_ref[r, k * feat : (k + 1) * feat] = x_ref[:, tile_cols(t, width)]
    for s in range(slots):
        if s % (slots // LOADS) == 0:
            loads[s // (slots // LOADS)].wait()
        dy = dy_ref[:, tile_cols(mine_ref[slots + s], width)]
        term = jnp.dot(dy, a_ref[s], preferred_element_type=jnp.float32)
        for lanes, half in enumerate(term_ref):
            half[s * feat : (s + 1) * feat] = term[:, lanes * LANES : (lanes + 1) * LANES]
    for r in range(peers):
        for lanes, half in enumerate(term_ref):
            of_feature = half[pl.ds(r, slots, stride=feat)].astype(out_ref.dtype)
            out_ref[r, most * feat :, lanes * LANES : (lanes + 1) * LANES] = of_feature


def h_kernel(
    mine_ref, asked_ref, cols_ref, counts_ref, in_ref, a_ref,
    out_hbm, acc_ref, pick_ref, sum_ref, out_ref, out_sem,
):
    slots = a_ref.shape[0]
    peers, most = out_ref.shape[0], PAIR_MOST
    row_tiles, feat, width = acc_ref.shape
    sums = [jnp.zeros((feat, width), jnp.float32) for _ in range(row_tiles)]
    for s in range(slots):
        held = jnp.maximum(mine_ref[s], 0)
        row = mine_ref[slots + s]
        x = in_ref[held // most, pl.ds(pl.multiple_of(held % most * feat, feat), feat)]
        term = lax.dot_general(x, a_ref[s], (((1,), (1,)), ((), ())), preferred_element_type=jnp.float32)
        for t in range(row_tiles):
            sums[t] = sums[t] + jnp.where((row == t) & (mine_ref[s] >= 0), term, 0.0)
    for t in range(row_tiles):
        acc_ref[t] = sums[t].astype(acc_ref.dtype)
    cols = cols_ref[...]
    live = lax.broadcasted_iota(jnp.int32, cols.shape, 0) < counts_ref[...]
    cols = jnp.where(live, cols, -1)
    tile_ids = lax.broadcasted_iota(jnp.int32, (slots, peers * row_tiles), 1)
    for r in range(peers):
        pick_ref[r * slots : (r + 1) * slots] = (cols[:, r : r + 1] == tile_ids).astype(pick_ref.dtype)
    terms = in_ref[:, most * feat :].reshape(peers * slots, width)
    sum_ref[: peers * row_tiles] = lax.dot_general(
        pick_ref[...], terms, (((0,), (0,)), ((), ())), preferred_element_type=jnp.float32
    )
    sum_ref[peers * row_tiles :] = jnp.zeros((row_tiles, width), jnp.float32)
    stores = []
    for r in range(peers):
        for k in range(most):
            out_ref[r, k * feat : (k + 1) * feat] = acc_ref[jnp.maximum(asked_ref[k, r] - 1, 0)]
        of_tiles = sum_ref[r * row_tiles : (r + 2) * row_tiles]
        out_ref[r, most * feat :] = of_tiles.astype(out_ref.dtype)
        if (r + 1) % (peers // STORES) == 0:
            part = pl.ds(r + 1 - peers // STORES, peers // STORES)
            copy = pltpu.make_async_copy(out_ref.at[part], out_hbm.at[part], out_sem.at[len(stores)])
            copy.start()
            stores.append(copy)
    for copy in stores:
        copy.wait()


def turn_kernel(own_ref, in0_ref, in1_ref, in2_ref, in3_ref, out0_ref, out1_ref, out2_ref, out3_ref):
    for e, out_ref in enumerate((out0_ref, out1_ref, out2_ref, out3_ref)):
        for g, in_ref in enumerate((in0_ref, in1_ref, in2_ref, in3_ref)):
            out_ref[g] = in_ref[own_ref[1] % GROUP ^ e]


def order_kernel(own_ref, in0_ref, in1_ref, in2_ref, in3_ref, out_ref):
    for e, in_ref in enumerate((in0_ref, in1_ref, in2_ref, in3_ref)):
        for g in range(GROUP):
            out_ref[own_ref[1] ^ (g * GROUP + e)] = in_ref[g]


def fill_kernel(mine_ref, in_ref, z_ref):
    slots, _, feat, _ = z_ref.shape
    for s in range(slots):
        held = jnp.maximum(mine_ref[s], 0)
        z_ref[s, 1] = in_ref[held // PAIR_MOST, pl.ds(pl.multiple_of(held % PAIR_MOST * feat, feat), feat)]


def join_kernel(mine_ref, in_ref, part_ref, z_ref, rows_ref, g_ref, sem):
    del part_ref
    peers, most = in_ref.shape[0], PAIR_MOST
    slots = z_ref.shape[0]
    row_tiles, feat, _ = g_ref.shape
    copies = []
    for s in range(slots):
        held = jnp.maximum(mine_ref[s], 0)
        tile = in_ref.at[held // most, pl.ds(pl.multiple_of(held % most * feat, feat), feat)]
        copies.append(pltpu.make_async_copy(tile, z_ref.at[s, 2], sem.at[s]))
        copies[s].start()
    step = in_ref.shape[1] - most * feat
    for r in range(peers):
        of_tiles = in_ref[r, most * feat :].astype(jnp.float32)
        for lanes, half in enumerate(rows_ref):
            half[r * step : (r + 1) * step] = of_tiles[:, lanes * LANES : (lanes + 1) * LANES]
    for t in range(row_tiles):
        for lanes, half in enumerate(rows_ref):
            of_tile = half[pl.ds(t, feat, stride=step)].astype(g_ref.dtype)
            g_ref[t, :, lanes * LANES : (lanes + 1) * LANES] = of_tile
    for s in range(slots):
        copies.append(pltpu.make_async_copy(g_ref.at[mine_ref[slots + s]], z_ref.at[s, 0], sem.at[slots + s]))
        copies[slots + s].start()
    for copy in copies:
        copy.wait()


def exchange(value, axis):
    return lax.all_to_all(value, axis, 0, 0, tiled=True)


def swap(value, step):
    if step == 0:
        return value
    places = range(lax.axis_size("depth"))
    return lax.ppermute(value, "depth", [(place, place ^ step) for place in places])


def hbm(kind):
    return pltpu.HBM(kind.shape, kind.dtype)


def far(value):
    return pltpu.with_memory_space_constraint(value, pltpu.HBM)


def near(value):
    return pltpu.with_memory_space_constraint(value, pltpu.VMEM)


def body(node_feat, grad_out, adjacency, tile_count, tile_row, tile_col):
    slots, width = adjacency.shape[0], adjacency.shape[1]
    feat = node_feat.shape[0]
    row_tiles = node_feat.shape[1] // width
    own_index = lax.axis_index("rows")
    peers = lax.axis_size("rows")
    bf16 = node_feat.dtype
    wanted_rows = PAIR_MOST * feat
    xg_type = jax.ShapeDtypeStruct((peers, wanted_rows + slots, width), bf16)
    hg_type = jax.ShapeDtypeStruct((peers, wanted_rows + 2 * row_tiles, width), bf16)
    asked_type = jax.ShapeDtypeStruct((PAIR_MOST, peers), jnp.int32)
    mine_type = jax.ShapeDtypeStruct((2 * slots,), jnp.int32)
    z_type = jax.ShapeDtypeStruct((slots, 3, feat, width), bf16)
    tiles = pltpu.VMEM((row_tiles, feat, width), bf16)
    slot_type = jax.ShapeDtypeStruct((slots, feat, width), bf16)
    node_feat, grad_out, adjacency = far(node_feat), far(grad_out), far(adjacency)
    cols, counts = tile_col.T, tile_count[None]

    four_type = jax.ShapeDtypeStruct((GROUP, feat, width), bf16)
    own = jnp.stack([own_index, lax.axis_index("depth")])
    xg_out, asked, mine, *dy_parts = pl.pallas_call(
        send_xg_kernel,
        out_shape=(hbm(xg_type), hbm(asked_type), hbm(mine_type)) + (hbm(four_type),) * GROUP,
        in_specs=[SMEM, SMEM, SMEM, SMEM, VMEM, VMEM, VMEM, VMEM, ANY],
        out_specs=(VMEM, SMEM, SMEM) + (VMEM,) * GROUP,
        compiler_params=PARAMS,
        scratch_shapes=[
            pltpu.VMEM(adjacency.shape, bf16),
            [pltpu.VMEM((slots * feat, LANES), jnp.float32)] * (width // LANES),
            pltpu.VMEM(asked_type.shape, jnp.int32),
            pltpu.SemaphoreType.DMA((LOADS,)),
            pltpu.SemaphoreType.DMA,
        ],
    )(
        own, far(cols), far(tile_row.T), far(tile_count), far(cols), far(counts),
        node_feat, grad_out, adjacency,
    )
    xg_in = exchange(xg_out, "rows")
    dy_parts = [swap(part, GROUP * step) for step, part in enumerate(dy_parts)]
    hg_out = pl.pallas_call(
        h_kernel,
        out_shape=hbm(hg_type),
        in_specs=[SMEM, SMEM, VMEM, VMEM, VMEM, VMEM],
        out_specs=HBM,
        compiler_params=PARAMS,
        scratch_shapes=[
            tiles,
            pltpu.VMEM((peers * slots, peers * row_tiles), bf16),
            pltpu.VMEM(((peers + 1) * row_tiles, width), jnp.float32),
            pltpu.VMEM(hg_type.shape, bf16),
            pltpu.SemaphoreType.DMA((STORES,)),
        ],
    )(far(mine), far(asked), near(cols), near(counts), near(xg_in), near(adjacency))
    hg_out, *dy_parts = lax.optimization_barrier((hg_out, *dy_parts))
    hg_in = exchange(hg_out, "rows")
    dy_parts = pl.pallas_call(
        turn_kernel,
        out_shape=(hbm(four_type),) * GROUP,
        in_specs=[SMEM] + [VMEM] * GROUP,
        out_specs=(VMEM,) * GROUP,
        compiler_params=PARAMS,
    )(own, *dy_parts)
    dy_parts = [swap(part, step) for step, part in enumerate(dy_parts)]
    z_part = pl.pallas_call(
        fill_kernel,
        out_shape=z_type,
        in_specs=[SMEM, VMEM],
        out_specs=VMEM,
        compiler_params=PARAMS,
    )(mine, near(xg_in))
    z_out = pl.pallas_call(
        join_kernel,
        out_shape=z_type,
        in_specs=[SMEM, VMEM, HBM],
        out_specs=HBM,
        compiler_params=PARAMS,
        input_output_aliases={2: 0},
        scratch_shapes=[
            [pltpu.VMEM((peers * 2 * row_tiles, LANES), jnp.float32)] * (width // LANES),
            tiles,
            pltpu.SemaphoreType.DMA((2 * slots,)),
        ],
    )(mine, near(hg_in), z_part)
    z_out, *dy_parts = lax.optimization_barrier((z_out, *dy_parts))
    dy = pl.pallas_call(
        order_kernel,
        out_shape=slot_type,
        in_specs=[SMEM] + [VMEM] * GROUP,
        out_specs=VMEM,
        compiler_params=PARAMS,
    )(own, *dy_parts)
    z_in = exchange(z_out, "depth")
    result = jnp.einsum("qfa,qfb->ab", dy, z_in[:, 2], preferred_element_type=jnp.float32)
    result += jnp.einsum("qfa,qfb->ab", z_in[:, 0], z_in[:, 1], preferred_element_type=jnp.float32)
    count = lax.dynamic_index_in_dim(tile_count, own_index, 0, keepdims=False)
    return jnp.where(lax.axis_index("depth") < count, result, 0.0)[None, None]


def solution(mesh):
    in_specs = (P("depth", "rows"), P("depth", "rows"), P("rows", None, None), P(), P(), P())
    out_specs = P("rows", "depth", None, None)
    return jax.shard_map(body, mesh=mesh, in_specs=in_specs, out_specs=out_specs, check_vma=False)
```

```python
import jax
import jax.numpy as jnp
from jax import lax
from jax.experimental import pallas as pl
from jax.experimental.pallas import tpu as pltpu
from jax.sharding import PartitionSpec as P

PAIR_MOST = 2
LOADS = 4
STORES = 4
LANES = 128
GROUP = 4
SMEM = pl.BlockSpec(memory_space=pltpu.SMEM)
VMEM = pl.BlockSpec(memory_space=pltpu.VMEM)
ANY = pl.BlockSpec(memory_space=pl.ANY)
HBM = pl.BlockSpec(memory_space=pltpu.HBM)
PARAMS = pltpu.CompilerParams(vmem_limit_bytes=12 * 2**20)


def tile_cols(index, width):
    return pl.ds(pl.multiple_of(index * width, width), width)


def send_xg_kernel(
    own_ref, col_ref, row_ref, count_ref, cols_ref, counts_ref, x_ref, dy_ref, a_hbm,
    out_hbm, asked_ref, mine_ref, dy0_ref, dy1_ref, dy2_ref, dy3_ref, out_ref, a_ref, term_ref, code_ref, a_sem, code_sem, out_sem,
):
    slots, width = a_ref.shape[0], a_ref.shape[1]
    peers, most = out_ref.shape[0], PAIR_MOST
    feat = x_ref.shape[0]
    row_tiles = x_ref.shape[1] // width
    loads = []
    for c in range(LOADS):
        part = pl.ds(c * (slots // LOADS), slots // LOADS)
        loads.append(pltpu.make_async_copy(a_hbm.at[part], a_ref.at[part], a_sem.at[c]))
        loads[c].start()
    own = own_ref[0]
    cols = cols_ref[...]
    slot_ids = lax.broadcasted_iota(jnp.int32, cols.shape, 0)
    wanted = (slot_ids < counts_ref[...]) & (cols // row_tiles == own)
    code = cols % row_tiles + 1
    first = jnp.max(jnp.where(wanted, (slots - 1 - slot_ids) * 8 + code, 0), axis=0, keepdims=True)
    last = jnp.max(jnp.where(wanted, slot_ids * 8 + code, 0), axis=0, keepdims=True)
    two = first // 8 + last // 8 != slots - 1
    code_ref[0:1] = first % 8
    code_ref[1:2] = jnp.where(two, last % 8, 0)
    to_scalars = pltpu.make_async_copy(code_ref, asked_ref, code_sem)
    to_scalars.start()
    owners = [col_ref[s, own] // row_tiles for s in range(slots)]
    for s in range(slots):
        row = row_ref[s, own]
        rank = jnp.int32(0)
        for earlier in range(s):
            rank = rank + jnp.where(owners[earlier] == owners[s], 1, 0)
        mine_ref[s] = jnp.where(s < count_ref[own], owners[s] * most + rank, -1)
        mine_ref[slots + s] = row
    for step, part_ref in enumerate((dy0_ref, dy1_ref, dy2_ref, dy3_ref)):
        group = own_ref[1] // GROUP ^ step
        for e in range(GROUP):
            part_ref[e] = dy_ref[:, tile_cols(row_ref[group * GROUP + e, own], width)]
    to_scalars.wait()
    for r in range(peers):
        for k in range(most):
            t = jnp.maximum(asked_ref[k, r] - 1, 0)
            out_ref[r, k * feat : (k + 1) * feat] = x_ref[:, tile_cols(t, width)]
    x_rows, g_rows = pl.ds(0, most * feat), pl.ds(most * feat, slots)
    stores = [
        pltpu.make_async_copy(out_ref.at[:, rows], out_hbm.at[:, rows], out_sem.at[k])
        for k, rows in enumerate((x_rows, g_rows))
    ]
    stores[0].start()
    for s in range(slots):
        if s % (slots // LOADS) == 0:
            loads[s // (slots // LOADS)].wait()
        dy = dy_ref[:, tile_cols(mine_ref[slots + s], width)]
        term = jnp.dot(dy, a_ref[s], preferred_element_type=jnp.float32)
        for lanes, half in enumerate(term_ref):
            half[s * feat : (s + 1) * feat] = term[:, lanes * LANES : (lanes + 1) * LANES]
    for r in range(peers):
        for lanes, half in enumerate(term_ref):
            of_feature = half[pl.ds(r, slots, stride=feat)].astype(out_ref.dtype)
            out_ref[r, most * feat :, lanes * LANES : (lanes + 1) * LANES] = of_feature
    stores[1].start()
    for store in stores:
        store.wait()


def h_kernel(
    mine_ref, asked_ref, cols_ref, counts_ref, in_ref, a_ref,
    out_hbm, z_ref, acc_ref, pick_ref, sum_ref, out_ref, out_sem, x_sem,
):
    slots = a_ref.shape[0]
    peers, most = out_ref.shape[0], PAIR_MOST
    row_tiles, feat, width = acc_ref.shape
    sums = [jnp.zeros((feat, width), jnp.float32) for _ in range(row_tiles)]
    stores = []
    for s in range(slots):
        held = jnp.maximum(mine_ref[s], 0)
        row = mine_ref[slots + s]
        place = pl.ds(pl.multiple_of(held % most * feat, feat), feat)
        x = in_ref[held // most, place]
        stores.append(pltpu.make_async_copy(in_ref.at[held // most, place], z_ref.at[s, 1], x_sem.at[s]))
        stores[s].start()
        term = lax.dot_general(x, a_ref[s], (((1,), (1,)), ((), ())), preferred_element_type=jnp.float32)
        for t in range(row_tiles):
            sums[t] = sums[t] + jnp.where((row == t) & (mine_ref[s] >= 0), term, 0.0)
    for t in range(row_tiles):
        acc_ref[t] = sums[t].astype(acc_ref.dtype)
    cols = cols_ref[...]
    live = lax.broadcasted_iota(jnp.int32, cols.shape, 0) < counts_ref[...]
    cols = jnp.where(live, cols, -1)
    tile_ids = lax.broadcasted_iota(jnp.int32, (slots, peers * row_tiles), 1)
    for r in range(peers):
        pick_ref[r * slots : (r + 1) * slots] = (cols[:, r : r + 1] == tile_ids).astype(pick_ref.dtype)
    terms = in_ref[:, most * feat :].reshape(peers * slots, width)
    sum_ref[: peers * row_tiles] = lax.dot_general(
        pick_ref[...], terms, (((0,), (0,)), ((), ())), preferred_element_type=jnp.float32
    )
    sum_ref[peers * row_tiles :] = jnp.zeros((row_tiles, width), jnp.float32)
    for r in range(peers):
        for k in range(most):
            out_ref[r, k * feat : (k + 1) * feat] = acc_ref[jnp.maximum(asked_ref[k, r] - 1, 0)]
        of_tiles = sum_ref[r * row_tiles : (r + 2) * row_tiles]
        out_ref[r, most * feat :] = of_tiles.astype(out_ref.dtype)
        if (r + 1) % (peers // STORES) == 0:
            part = pl.ds(r + 1 - peers // STORES, peers // STORES)
            copy = pltpu.make_async_copy(out_ref.at[part], out_hbm.at[part], out_sem.at[len(stores) - slots])
            copy.start()
            stores.append(copy)
    for copy in stores:
        copy.wait()


def turn_kernel(own_ref, in0_ref, in1_ref, in2_ref, in3_ref, out0_ref, out1_ref, out2_ref, out3_ref):
    for e, out_ref in enumerate((out0_ref, out1_ref, out2_ref, out3_ref)):
        for g, in_ref in enumerate((in0_ref, in1_ref, in2_ref, in3_ref)):
            out_ref[g] = in_ref[own_ref[1] % GROUP ^ e]


def order_kernel(own_ref, in0_ref, in1_ref, in2_ref, in3_ref, out_ref):
    for e, in_ref in enumerate((in0_ref, in1_ref, in2_ref, in3_ref)):
        for g in range(GROUP):
            out_ref[own_ref[1] ^ (g * GROUP + e)] = in_ref[g]


def join_kernel(mine_ref, in_ref, part_ref, z_ref, rows_ref, g_ref, sem):
    del part_ref
    peers, most = in_ref.shape[0], PAIR_MOST
    slots = z_ref.shape[0]
    row_tiles, feat, _ = g_ref.shape
    copies = []
    for s in range(slots):
        held = jnp.maximum(mine_ref[s], 0)
        tile = in_ref.at[held // most, pl.ds(pl.multiple_of(held % most * feat, feat), feat)]
        copies.append(pltpu.make_async_copy(tile, z_ref.at[s, 2], sem.at[s]))
        copies[s].start()
    step = in_ref.shape[1] - most * feat
    for r in range(peers):
        of_tiles = in_ref[r, most * feat :].astype(jnp.float32)
        for lanes, half in enumerate(rows_ref):
            half[r * step : (r + 1) * step] = of_tiles[:, lanes * LANES : (lanes + 1) * LANES]
    for t in range(row_tiles):
        for lanes, half in enumerate(rows_ref):
            of_tile = half[pl.ds(t, feat, stride=step)].astype(g_ref.dtype)
            g_ref[t, :, lanes * LANES : (lanes + 1) * LANES] = of_tile
    for s in range(slots):
        copies.append(pltpu.make_async_copy(g_ref.at[mine_ref[slots + s]], z_ref.at[s, 0], sem.at[slots + s]))
        copies[slots + s].start()
    for copy in copies:
        copy.wait()


def exchange(value, axis):
    return lax.all_to_all(value, axis, 0, 0, tiled=True)


def swap(value, step):
    if step == 0:
        return value
    places = range(lax.axis_size("depth"))
    return lax.ppermute(value, "depth", [(place, place ^ step) for place in places])


def hbm(kind):
    return pltpu.HBM(kind.shape, kind.dtype)


def far(value):
    return pltpu.with_memory_space_constraint(value, pltpu.HBM)


def near(value):
    return pltpu.with_memory_space_constraint(value, pltpu.VMEM)


def body(node_feat, grad_out, adjacency, tile_count, tile_row, tile_col):
    slots, width = adjacency.shape[0], adjacency.shape[1]
    feat = node_feat.shape[0]
    row_tiles = node_feat.shape[1] // width
    own_index = lax.axis_index("rows")
    peers = lax.axis_size("rows")
    bf16 = node_feat.dtype
    wanted_rows = PAIR_MOST * feat
    xg_type = jax.ShapeDtypeStruct((peers, wanted_rows + slots, width), bf16)
    hg_type = jax.ShapeDtypeStruct((peers, wanted_rows + 2 * row_tiles, width), bf16)
    asked_type = jax.ShapeDtypeStruct((PAIR_MOST, peers), jnp.int32)
    mine_type = jax.ShapeDtypeStruct((2 * slots,), jnp.int32)
    z_type = jax.ShapeDtypeStruct((slots, 3, feat, width), bf16)
    tiles = pltpu.VMEM((row_tiles, feat, width), bf16)
    slot_type = jax.ShapeDtypeStruct((slots, feat, width), bf16)
    node_feat, grad_out, adjacency = far(node_feat), far(grad_out), far(adjacency)
    cols, counts = tile_col.T, tile_count[None]

    four_type = jax.ShapeDtypeStruct((GROUP, feat, width), bf16)
    own = jnp.stack([own_index, lax.axis_index("depth")])
    xg_out, asked, mine, *dy_parts = pl.pallas_call(
        send_xg_kernel,
        out_shape=(hbm(xg_type), hbm(asked_type), hbm(mine_type)) + (hbm(four_type),) * GROUP,
        in_specs=[SMEM, SMEM, SMEM, SMEM, VMEM, VMEM, VMEM, VMEM, ANY],
        out_specs=(HBM, SMEM, SMEM) + (VMEM,) * GROUP,
        compiler_params=PARAMS,
        scratch_shapes=[
            pltpu.VMEM(xg_type.shape, bf16),
            pltpu.VMEM(adjacency.shape, bf16),
            [pltpu.VMEM((slots * feat, LANES), jnp.float32)] * (width // LANES),
            pltpu.VMEM(asked_type.shape, jnp.int32),
            pltpu.SemaphoreType.DMA((LOADS,)),
            pltpu.SemaphoreType.DMA,
            pltpu.SemaphoreType.DMA((2,)),
        ],
    )(
        own, far(cols), far(tile_row.T), far(tile_count), far(cols), far(counts),
        node_feat, grad_out, adjacency,
    )
    xg_in = exchange(xg_out, "rows")
    dy_parts = [swap(part, GROUP * step) for step, part in enumerate(dy_parts)]
    hg_out, z_part = pl.pallas_call(
        h_kernel,
        out_shape=(hbm(hg_type), hbm(z_type)),
        in_specs=[SMEM, SMEM, VMEM, VMEM, VMEM, VMEM],
        out_specs=(HBM, HBM),
        compiler_params=PARAMS,
        scratch_shapes=[
            tiles,
            pltpu.VMEM((peers * slots, peers * row_tiles), bf16),
            pltpu.VMEM(((peers + 1) * row_tiles, width), jnp.float32),
            pltpu.VMEM(hg_type.shape, bf16),
            pltpu.SemaphoreType.DMA((STORES,)),
            pltpu.SemaphoreType.DMA((slots,)),
        ],
    )(far(mine), far(asked), near(cols), near(counts), near(xg_in), near(adjacency))
    hg_out, *dy_parts = lax.optimization_barrier((hg_out, *dy_parts))
    hg_in = exchange(hg_out, "rows")
    dy_parts = pl.pallas_call(
        turn_kernel,
        out_shape=(hbm(four_type),) * GROUP,
        in_specs=[SMEM] + [VMEM] * GROUP,
        out_specs=(VMEM,) * GROUP,
        compiler_params=PARAMS,
    )(own, *dy_parts)
    dy_parts = [swap(part, step) for step, part in enumerate(dy_parts)]
    z_out = pl.pallas_call(
        join_kernel,
        out_shape=z_type,
        in_specs=[SMEM, VMEM, HBM],
        out_specs=HBM,
        compiler_params=PARAMS,
        input_output_aliases={2: 0},
        scratch_shapes=[
            [pltpu.VMEM((peers * 2 * row_tiles, LANES), jnp.float32)] * (width // LANES),
            tiles,
            pltpu.SemaphoreType.DMA((2 * slots,)),
        ],
    )(mine, near(hg_in), z_part)
    z_out, *dy_parts = lax.optimization_barrier((z_out, *dy_parts))
    dy = pl.pallas_call(
        order_kernel,
        out_shape=slot_type,
        in_specs=[SMEM] + [VMEM] * GROUP,
        out_specs=VMEM,
        compiler_params=PARAMS,
    )(own, *dy_parts)
    z_in = exchange(z_out, "depth")
    result = jnp.einsum("qfa,qfb->ab", dy, z_in[:, 2], preferred_element_type=jnp.float32)
    result += jnp.einsum("qfa,qfb->ab", z_in[:, 0], z_in[:, 1], preferred_element_type=jnp.float32)
    count = lax.dynamic_index_in_dim(tile_count, own_index, 0, keepdims=False)
    return jnp.where(lax.axis_index("depth") < count, result, 0.0)[None, None]


def solution(mesh):
    in_specs = (P("depth", "rows"), P("depth", "rows"), P("rows", None, None), P(), P(), P())
    out_specs = P("rows", "depth", None, None)
    return jax.shard_map(body, mesh=mesh, in_specs=in_specs, out_specs=out_specs, check_vma=False)
```

```python
import jax
import jax.numpy as jnp
from jax import lax
from jax.experimental import pallas as pl
from jax.experimental.pallas import tpu as pltpu
from jax.sharding import PartitionSpec as P

PAIR_MOST = 2
LOADS = 4
STORES = 4
LANES = 128
GROUP = 4
SMEM = pl.BlockSpec(memory_space=pltpu.SMEM)
VMEM = pl.BlockSpec(memory_space=pltpu.VMEM)
ANY = pl.BlockSpec(memory_space=pl.ANY)
HBM = pl.BlockSpec(memory_space=pltpu.HBM)
PARAMS = pltpu.CompilerParams(vmem_limit_bytes=12 * 2**20)


def tile_cols(index, width):
    return pl.ds(pl.multiple_of(index * width, width), width)


def send_xg_kernel(
    own_ref, col_ref, row_ref, count_ref, cols_ref, counts_ref, x_ref, dy_ref, a_hbm,
    out_ref, asked_ref, mine_ref, dy0_ref, dy1_ref, dy2_ref, dy3_ref, a_ref, term_ref, code_ref, a_sem, code_sem,
):
    slots, width = a_ref.shape[0], a_ref.shape[1]
    peers, most = out_ref.shape[0], PAIR_MOST
    feat = x_ref.shape[0]
    row_tiles = x_ref.shape[1] // width
    loads = []
    for c in range(LOADS):
        part = pl.ds(c * (slots // LOADS), slots // LOADS)
        loads.append(pltpu.make_async_copy(a_hbm.at[part], a_ref.at[part], a_sem.at[c]))
        loads[c].start()
    own = own_ref[0]
    cols = cols_ref[...]
    slot_ids = lax.broadcasted_iota(jnp.int32, cols.shape, 0)
    wanted = (slot_ids < counts_ref[...]) & (cols // row_tiles == own)
    code = cols % row_tiles + 1
    first = jnp.max(jnp.where(wanted, (slots - 1 - slot_ids) * 8 + code, 0), axis=0, keepdims=True)
    last = jnp.max(jnp.where(wanted, slot_ids * 8 + code, 0), axis=0, keepdims=True)
    two = first // 8 + last // 8 != slots - 1
    code_ref[0:1] = first % 8
    code_ref[1:2] = jnp.where(two, last % 8, 0)
    to_scalars = pltpu.make_async_copy(code_ref, asked_ref, code_sem)
    to_scalars.start()
    owners = [col_ref[s, own] // row_tiles for s in range(slots)]
    for s in range(slots):
        row = row_ref[s, own]
        rank = jnp.int32(0)
        for earlier in range(s):
            rank = rank + jnp.where(owners[earlier] == owners[s], 1, 0)
        mine_ref[s] = jnp.where(s < count_ref[own], owners[s] * most + rank, -1)
        mine_ref[slots + s] = row
    for step, part_ref in enumerate((dy0_ref, dy1_ref, dy2_ref, dy3_ref)):
        group = own_ref[1] // GROUP ^ step
        for e in range(GROUP):
            part_ref[e] = dy_ref[:, tile_cols(row_ref[group * GROUP + e, own], width)]
    to_scalars.wait()
    for r in range(peers):
        for k in range(most):
            t = jnp.maximum(asked_ref[k, r] - 1, 0)
            out_ref[r, k * feat : (k + 1) * feat] = x_ref[:, tile_cols(t, width)]
    for s in range(slots):
        if s % (slots // LOADS) == 0:
            loads[s // (slots // LOADS)].wait()
        dy = dy_ref[:, tile_cols(mine_ref[slots + s], width)]
        term = jnp.dot(dy, a_ref[s], preferred_element_type=jnp.float32)
        for lanes, half in enumerate(term_ref):
            half[s * feat : (s + 1) * feat] = term[:, lanes * LANES : (lanes + 1) * LANES]
    for r in range(peers):
        for lanes, half in enumerate(term_ref):
            of_feature = half[pl.ds(r, slots, stride=feat)].astype(out_ref.dtype)
            out_ref[r, most * feat :, lanes * LANES : (lanes + 1) * LANES] = of_feature


def h_kernel(
    mine_ref, asked_ref, cols_ref, counts_ref, in_ref, a_ref,
    out_hbm, acc_ref, pick_ref, sum_ref, out_ref, out_sem,
):
    slots = a_ref.shape[0]
    peers, most = out_ref.shape[0], PAIR_MOST
    row_tiles, feat, width = acc_ref.shape
    sums = [jnp.zeros((feat, width), jnp.float32) for _ in range(row_tiles)]
    for s in range(slots):
        held = jnp.maximum(mine_ref[s], 0)
        row = mine_ref[slots + s]
        x = in_ref[held // most, pl.ds(pl.multiple_of(held % most * feat, feat), feat)]
        term = lax.dot_general(x, a_ref[s], (((1,), (1,)), ((), ())), preferred_element_type=jnp.float32)
        for t in range(row_tiles):
            sums[t] = sums[t] + jnp.where((row == t) & (mine_ref[s] >= 0), term, 0.0)
    for t in range(row_tiles):
        acc_ref[t] = sums[t].astype(acc_ref.dtype)
    cols = cols_ref[...]
    live = lax.broadcasted_iota(jnp.int32, cols.shape, 0) < counts_ref[...]
    cols = jnp.where(live, cols, -1)
    tile_ids = lax.broadcasted_iota(jnp.int32, (slots, peers * row_tiles), 1)
    for r in range(peers):
        pick_ref[r * slots : (r + 1) * slots] = (cols[:, r : r + 1] == tile_ids).astype(pick_ref.dtype)
    terms = in_ref[:, most * feat :].reshape(peers * slots, width)
    sum_ref[: peers * row_tiles] = lax.dot_general(
        pick_ref[...], terms, (((0,), (0,)), ((), ())), preferred_element_type=jnp.float32
    )
    sum_ref[peers * row_tiles :] = jnp.zeros((row_tiles, width), jnp.float32)
    stores = []
    for r in range(peers):
        for k in range(most):
            out_ref[r, k * feat : (k + 1) * feat] = acc_ref[jnp.maximum(asked_ref[k, r] - 1, 0)]
        of_tiles = sum_ref[r * row_tiles : (r + 2) * row_tiles]
        out_ref[r, most * feat :] = of_tiles.astype(out_ref.dtype)
        if (r + 1) % (peers // STORES) == 0:
            part = pl.ds(r + 1 - peers // STORES, peers // STORES)
            copy = pltpu.make_async_copy(out_ref.at[part], out_hbm.at[part], out_sem.at[len(stores)])
            copy.start()
            stores.append(copy)
    for copy in stores:
        copy.wait()


def turn_kernel(own_ref, in0_ref, in1_ref, in2_ref, in3_ref, out0_ref, out1_ref, out2_ref, out3_ref):
    for e, out_ref in enumerate((out0_ref, out1_ref, out2_ref, out3_ref)):
        for g, in_ref in enumerate((in0_ref, in1_ref, in2_ref, in3_ref)):
            out_ref[g] = in_ref[own_ref[1] % GROUP ^ e]


def order_kernel(own_ref, in0_ref, in1_ref, in2_ref, in3_ref, out_ref):
    for e, in_ref in enumerate((in0_ref, in1_ref, in2_ref, in3_ref)):
        for g in range(GROUP):
            out_ref[own_ref[1] ^ (g * GROUP + e)] = in_ref[g]


def fill_kernel(mine_ref, in_ref, z_ref):
    slots, _, feat, _ = z_ref.shape
    for s in range(slots):
        held = jnp.maximum(mine_ref[s], 0)
        z_ref[s, 1] = in_ref[held // PAIR_MOST, pl.ds(pl.multiple_of(held % PAIR_MOST * feat, feat), feat)]


def join_kernel(mine_ref, in_ref, part_ref, z_ref, rows_ref, g_ref, sem):
    del part_ref
    peers, most = in_ref.shape[0], PAIR_MOST
    slots = z_ref.shape[0]
    row_tiles, feat, _ = g_ref.shape
    copies = []
    for s in range(slots):
        held = jnp.maximum(mine_ref[s], 0)
        tile = in_ref.at[held // most, pl.ds(pl.multiple_of(held % most * feat, feat), feat)]
        copies.append(pltpu.make_async_copy(tile, z_ref.at[s, 2], sem.at[s]))
        copies[s].start()
    step = in_ref.shape[1] - most * feat
    for r in range(peers):
        of_tiles = in_ref[r, most * feat :].astype(jnp.float32)
        for lanes, half in enumerate(rows_ref):
            half[r * step : (r + 1) * step] = of_tiles[:, lanes * LANES : (lanes + 1) * LANES]
    for t in range(row_tiles):
        for lanes, half in enumerate(rows_ref):
            of_tile = half[pl.ds(t, feat, stride=step)].astype(g_ref.dtype)
            g_ref[t, :, lanes * LANES : (lanes + 1) * LANES] = of_tile
    for s in range(slots):
        copies.append(pltpu.make_async_copy(g_ref.at[mine_ref[slots + s]], z_ref.at[s, 0], sem.at[slots + s]))
        copies[slots + s].start()
    for copy in copies:
        copy.wait()


def exchange(value, axis):
    return lax.all_to_all(value, axis, 0, 0, tiled=True)


def swap(value, step):
    if step == 0:
        return value
    places = range(lax.axis_size("depth"))
    return lax.ppermute(value, "depth", [(place, place ^ step) for place in places])


def hbm(kind):
    return pltpu.HBM(kind.shape, kind.dtype)


def far(value):
    return pltpu.with_memory_space_constraint(value, pltpu.HBM)


def near(value):
    return pltpu.with_memory_space_constraint(value, pltpu.VMEM)


def body(node_feat, grad_out, adjacency, tile_count, tile_row, tile_col):
    slots, width = adjacency.shape[0], adjacency.shape[1]
    feat = node_feat.shape[0]
    row_tiles = node_feat.shape[1] // width
    own_index = lax.axis_index("rows")
    peers = lax.axis_size("rows")
    bf16 = node_feat.dtype
    wanted_rows = PAIR_MOST * feat
    xg_type = jax.ShapeDtypeStruct((peers, wanted_rows + slots, width), bf16)
    hg_type = jax.ShapeDtypeStruct((peers, wanted_rows + 2 * row_tiles, width), bf16)
    asked_type = jax.ShapeDtypeStruct((PAIR_MOST, peers), jnp.int32)
    mine_type = jax.ShapeDtypeStruct((2 * slots,), jnp.int32)
    z_type = jax.ShapeDtypeStruct((slots, 3, feat, width), bf16)
    tiles = pltpu.VMEM((row_tiles, feat, width), bf16)
    slot_type = jax.ShapeDtypeStruct((slots, feat, width), bf16)
    node_feat, grad_out, adjacency = far(node_feat), far(grad_out), far(adjacency)
    cols, counts = tile_col.T, tile_count[None]

    four_type = jax.ShapeDtypeStruct((GROUP, feat, width), bf16)
    own = jnp.stack([own_index, lax.axis_index("depth")])
    xg_out, asked, mine, *dy_parts = pl.pallas_call(
        send_xg_kernel,
        out_shape=(hbm(xg_type), hbm(asked_type), hbm(mine_type)) + (hbm(four_type),) * GROUP,
        in_specs=[SMEM, SMEM, SMEM, SMEM, VMEM, VMEM, VMEM, VMEM, ANY],
        out_specs=(VMEM, SMEM, SMEM) + (VMEM,) * GROUP,
        compiler_params=PARAMS,
        scratch_shapes=[
            pltpu.VMEM(adjacency.shape, bf16),
            [pltpu.VMEM((slots * feat, LANES), jnp.float32)] * (width // LANES),
            pltpu.VMEM(asked_type.shape, jnp.int32),
            pltpu.SemaphoreType.DMA((LOADS,)),
            pltpu.SemaphoreType.DMA,
        ],
    )(
        own, far(cols), far(tile_row.T), far(tile_count), far(cols), far(counts),
        node_feat, grad_out, adjacency,
    )
    xg_in = exchange(xg_out, "rows")
    dy_parts = [swap(part, GROUP * step) for step, part in enumerate(dy_parts)]
    hg_out = pl.pallas_call(
        h_kernel,
        out_shape=hbm(hg_type),
        in_specs=[SMEM, SMEM, VMEM, VMEM, VMEM, VMEM],
        out_specs=HBM,
        compiler_params=PARAMS,
        scratch_shapes=[
            tiles,
            pltpu.VMEM((peers * slots, peers * row_tiles), bf16),
            pltpu.VMEM(((peers + 1) * row_tiles, width), jnp.float32),
            pltpu.VMEM(hg_type.shape, bf16),
            pltpu.SemaphoreType.DMA((STORES,)),
        ],
    )(far(mine), far(asked), near(cols), near(counts), near(xg_in), near(adjacency))
    hg_in = exchange(hg_out, "rows")
    dy_parts = pl.pallas_call(
        turn_kernel,
        out_shape=(hbm(four_type),) * GROUP,
        in_specs=[SMEM] + [VMEM] * GROUP,
        out_specs=(VMEM,) * GROUP,
        compiler_params=PARAMS,
        cost_estimate=pl.CostEstimate(flops=int(5e10), bytes_accessed=0, transcendentals=0),
    )(own, *dy_parts)
    dy_parts = [swap(part, step) for step, part in enumerate(dy_parts)]
    z_part = pl.pallas_call(
        fill_kernel,
        out_shape=z_type,
        in_specs=[SMEM, VMEM],
        out_specs=VMEM,
        compiler_params=PARAMS,
    )(mine, near(xg_in))
    z_out = pl.pallas_call(
        join_kernel,
        out_shape=z_type,
        in_specs=[SMEM, VMEM, HBM],
        out_specs=HBM,
        compiler_params=PARAMS,
        input_output_aliases={2: 0},
        scratch_shapes=[
            [pltpu.VMEM((peers * 2 * row_tiles, LANES), jnp.float32)] * (width // LANES),
            tiles,
            pltpu.SemaphoreType.DMA((2 * slots,)),
        ],
    )(mine, near(hg_in), z_part)
    z_out, *dy_parts = lax.optimization_barrier((z_out, *dy_parts))
    dy = pl.pallas_call(
        order_kernel,
        out_shape=slot_type,
        in_specs=[SMEM] + [VMEM] * GROUP,
        out_specs=VMEM,
        compiler_params=PARAMS,
    )(own, *dy_parts)
    z_in = exchange(z_out, "depth")
    result = jnp.einsum("qfa,qfb->ab", dy, z_in[:, 2], preferred_element_type=jnp.float32)
    result += jnp.einsum("qfa,qfb->ab", z_in[:, 0], z_in[:, 1], preferred_element_type=jnp.float32)
    count = lax.dynamic_index_in_dim(tile_count, own_index, 0, keepdims=False)
    return jnp.where(lax.axis_index("depth") < count, result, 0.0)[None, None]


def solution(mesh):
    in_specs = (P("depth", "rows"), P("depth", "rows"), P("rows", None, None), P(), P(), P())
    out_specs = P("rows", "depth", None, None)
    return jax.shard_map(body, mesh=mesh, in_specs=in_specs, out_specs=out_specs, check_vma=False)
```

```python
import jax
import jax.numpy as jnp
from jax import lax
from jax.experimental import pallas as pl
from jax.experimental.pallas import tpu as pltpu
from jax.sharding import PartitionSpec as P

PAIR_MOST = 2
LOADS = 2
STORES = 4
LANES = 128
GROUP = 4
SMEM = pl.BlockSpec(memory_space=pltpu.SMEM)
VMEM = pl.BlockSpec(memory_space=pltpu.VMEM)
ANY = pl.BlockSpec(memory_space=pl.ANY)
HBM = pl.BlockSpec(memory_space=pltpu.HBM)
PARAMS = pltpu.CompilerParams(vmem_limit_bytes=12 * 2**20)


def tile_cols(index, width):
    return pl.ds(pl.multiple_of(index * width, width), width)


def send_xg_kernel(
    own_ref, col_hbm, row_hbm, count_hbm, counts_hbm, x_hbm, dy_hbm, a_hbm,
    out_ref, asked_ref, mine_ref, dy0_ref, dy1_ref, dy2_ref, dy3_ref,
    col_ref, row_ref, count_ref, cols_ref, counts_ref, x_ref, dy_ref,
    a_ref, term_ref, code_ref, load_sem, a_sem, code_sem,
):
    slots, width = a_ref.shape[0], a_ref.shape[1]
    peers, most = out_ref.shape[0], PAIR_MOST
    feat = x_ref.shape[0]
    row_tiles = x_ref.shape[1] // width
    small = [
        pltpu.make_async_copy(source, target, load_sem.at[k])
        for k, (source, target) in enumerate(
            (
                (col_hbm, cols_ref),
                (counts_hbm, counts_ref),
                (col_hbm, col_ref),
                (row_hbm, row_ref),
                (count_hbm, count_ref),
                (dy_hbm, dy_ref),
                (x_hbm, x_ref),
            )
        )
    ]
    for load in small:
        load.start()
    loads = []
    for c in range(LOADS):
        part = pl.ds(c * (slots // LOADS), slots // LOADS)
        loads.append(pltpu.make_async_copy(a_hbm.at[part], a_ref.at[part], a_sem.at[c]))
        loads[c].start()
    own = own_ref[0]
    for load in small[:2]:
        load.wait()
    cols = cols_ref[...]
    slot_ids = lax.broadcasted_iota(jnp.int32, cols.shape, 0)
    wanted = (slot_ids < counts_ref[...]) & (cols // row_tiles == own)
    code = cols % row_tiles + 1
    first = jnp.max(jnp.where(wanted, (slots - 1 - slot_ids) * 8 + code, 0), axis=0, keepdims=True)
    last = jnp.max(jnp.where(wanted, slot_ids * 8 + code, 0), axis=0, keepdims=True)
    two = first // 8 + last // 8 != slots - 1
    code_ref[0:1] = first % 8
    code_ref[1:2] = jnp.where(two, last % 8, 0)
    to_scalars = pltpu.make_async_copy(code_ref, asked_ref, code_sem)
    to_scalars.start()
    for load in small[2:]:
        load.wait()
    owners = [col_ref[s, own] // row_tiles for s in range(slots)]
    for s in range(slots):
        row = row_ref[s, own]
        rank = jnp.int32(0)
        for earlier in range(s):
            rank = rank + jnp.where(owners[earlier] == owners[s], 1, 0)
        mine_ref[s] = jnp.where(s < count_ref[own], owners[s] * most + rank, -1)
        mine_ref[slots + s] = row
    for step, part_ref in enumerate((dy0_ref, dy1_ref, dy2_ref, dy3_ref)):
        group = own_ref[1] // GROUP ^ step
        for e in range(GROUP):
            part_ref[e] = dy_ref[:, tile_cols(row_ref[group * GROUP + e, own], width)]
    to_scalars.wait()
    for r in range(peers):
        for k in range(most):
            t = jnp.maximum(asked_ref[k, r] - 1, 0)
            out_ref[r, k * feat : (k + 1) * feat] = x_ref[:, tile_cols(t, width)]
    for s in range(slots):
        if s % (slots // LOADS) == 0:
            loads[s // (slots // LOADS)].wait()
        dy = dy_ref[:, tile_cols(mine_ref[slots + s], width)]
        term = jnp.dot(dy, a_ref[s], preferred_element_type=jnp.float32)
        for lanes, half in enumerate(term_ref):
            half[s * feat : (s + 1) * feat] = term[:, lanes * LANES : (lanes + 1) * LANES]
    for r in range(peers):
        for lanes, half in enumerate(term_ref):
            of_feature = half[pl.ds(r, slots, stride=feat)].astype(out_ref.dtype)
            out_ref[r, most * feat :, lanes * LANES : (lanes + 1) * LANES] = of_feature


def h_kernel(
    mine_ref, asked_ref, cols_ref, counts_ref, in_ref, a_ref,
    out_hbm, acc_ref, pick_ref, sum_ref, out_ref, out_sem,
):
    slots = a_ref.shape[0]
    peers, most = out_ref.shape[0], PAIR_MOST
    row_tiles, feat, width = acc_ref.shape
    sums = [jnp.zeros((feat, width), jnp.float32) for _ in range(row_tiles)]
    for s in range(slots):
        held = jnp.maximum(mine_ref[s], 0)
        row = mine_ref[slots + s]
        x = in_ref[held // most, pl.ds(pl.multiple_of(held % most * feat, feat), feat)]
        term = lax.dot_general(x, a_ref[s], (((1,), (1,)), ((), ())), preferred_element_type=jnp.float32)
        for t in range(row_tiles):
            sums[t] = sums[t] + jnp.where((row == t) & (mine_ref[s] >= 0), term, 0.0)
    for t in range(row_tiles):
        acc_ref[t] = sums[t].astype(acc_ref.dtype)
    cols = cols_ref[...]
    live = lax.broadcasted_iota(jnp.int32, cols.shape, 0) < counts_ref[...]
    cols = jnp.where(live, cols, -1)
    tile_ids = lax.broadcasted_iota(jnp.int32, (slots, peers * row_tiles), 1)
    for r in range(peers):
        pick_ref[r * slots : (r + 1) * slots] = (cols[:, r : r + 1] == tile_ids).astype(pick_ref.dtype)
    terms = in_ref[:, most * feat :].reshape(peers * slots, width)
    sum_ref[...] = lax.dot_general(
        pick_ref[...], terms, (((0,), (0,)), ((), ())), preferred_element_type=jnp.float32
    )
    stores = []
    for r in range(peers):
        of_tiles = sum_ref[r * row_tiles : (r + 1) * row_tiles]
        halves = []
        for half in range(width // LANES):
            lanes = slice(half * LANES, (half + 1) * LANES)
            for k in range(most):
                first = (half * most + k) * feat
                out_ref[r, first : first + feat] = acc_ref[jnp.maximum(asked_ref[k, r] - 1, 0), :, lanes]
            halves.append(of_tiles[:, lanes])
        out_ref[r, width // LANES * most * feat :] = jnp.concatenate(halves).astype(out_ref.dtype)
        if (r + 1) % (peers // STORES) == 0:
            part = pl.ds(r + 1 - peers // STORES, peers // STORES)
            copy = pltpu.make_async_copy(out_ref.at[part], out_hbm.at[part], out_sem.at[len(stores)])
            copy.start()
            stores.append(copy)
    for copy in stores:
        copy.wait()


def turn_kernel(own_ref, in0_ref, in1_ref, in2_ref, in3_ref, out0_ref, out1_ref, out2_ref, out3_ref):
    for e, out_ref in enumerate((out0_ref, out1_ref, out2_ref, out3_ref)):
        for g, in_ref in enumerate((in0_ref, in1_ref, in2_ref, in3_ref)):
            out_ref[g] = in_ref[own_ref[1] % GROUP ^ e]


def order_kernel(own_ref, in0_ref, in1_ref, in2_ref, in3_ref, out_ref):
    for e, in_ref in enumerate((in0_ref, in1_ref, in2_ref, in3_ref)):
        for g in range(GROUP):
            out_ref[own_ref[1] ^ (g * GROUP + e)] = in_ref[g]


def fill_kernel(mine_ref, in_ref, z_ref):
    slots, _, feat, _ = z_ref.shape
    for s in range(slots):
        held = jnp.maximum(mine_ref[s], 0)
        z_ref[s, 1] = in_ref[held // PAIR_MOST, pl.ds(pl.multiple_of(held % PAIR_MOST * feat, feat), feat)]


def join_kernel(mine_ref, in_ref, part_ref, z_ref, rows_ref, g_ref, h_sem, g_sem):
    del part_ref
    peers, most = in_ref.shape[0], PAIR_MOST
    slots = z_ref.shape[0]
    row_tiles, feat, width = g_ref.shape
    halves = width // LANES
    copies = []
    for s in range(slots):
        held = jnp.maximum(mine_ref[s], 0)
        for half in range(halves):
            first = pl.multiple_of((half * most + held % most) * feat, feat)
            tile = in_ref.at[held // most, pl.ds(first, feat)]
            place = z_ref.at[s, 2, :, pl.ds(half * LANES, LANES)]
            copies.append(pltpu.make_async_copy(tile, place, h_sem.at[s * halves + half]))
            copies[-1].start()
    step = halves * row_tiles
    for r in range(peers):
        rows_ref[r * step : (r + 1) * step] = in_ref[r, halves * most * feat :].astype(jnp.float32)
    for t in range(row_tiles):
        for half in range(halves):
            of_tile = rows_ref[pl.ds(half * row_tiles + t, feat, stride=step)].astype(g_ref.dtype)
            g_ref[t, :, half * LANES : (half + 1) * LANES] = of_tile
    for s in range(slots):
        copies.append(pltpu.make_async_copy(g_ref.at[mine_ref[slots + s]], z_ref.at[s, 0], g_sem.at[s]))
        copies[-1].start()
    for copy in copies:
        copy.wait()


def exchange(value, axis):
    return lax.all_to_all(value, axis, 0, 0, tiled=True)


def swap(value, step):
    if step == 0:
        return value
    places = range(lax.axis_size("depth"))
    return lax.ppermute(value, "depth", [(place, place ^ step) for place in places])


def hbm(kind):
    return pltpu.HBM(kind.shape, kind.dtype)


def far(value):
    return pltpu.with_memory_space_constraint(value, pltpu.HBM)


def near(value):
    return pltpu.with_memory_space_constraint(value, pltpu.VMEM)


def body(node_feat, grad_out, adjacency, tile_count, tile_row, tile_col):
    slots, width = adjacency.shape[0], adjacency.shape[1]
    feat = node_feat.shape[0]
    row_tiles = node_feat.shape[1] // width
    own_index = lax.axis_index("rows")
    peers = lax.axis_size("rows")
    bf16 = node_feat.dtype
    wanted_rows = PAIR_MOST * feat
    xg_type = jax.ShapeDtypeStruct((peers, wanted_rows + slots, width), bf16)
    hg_type = jax.ShapeDtypeStruct((peers, (wanted_rows + row_tiles) * (width // LANES), LANES), bf16)
    asked_type = jax.ShapeDtypeStruct((PAIR_MOST, peers), jnp.int32)
    mine_type = jax.ShapeDtypeStruct((2 * slots,), jnp.int32)
    z_type = jax.ShapeDtypeStruct((slots, 3, feat, width), bf16)
    tiles = pltpu.VMEM((row_tiles, feat, width), bf16)
    slot_type = jax.ShapeDtypeStruct((slots, feat, width), bf16)
    node_feat, grad_out, adjacency = far(node_feat), far(grad_out), far(adjacency)
    cols, counts = tile_col.T, tile_count[None]

    four_type = jax.ShapeDtypeStruct((GROUP, feat, width), bf16)
    own = jnp.stack([own_index, lax.axis_index("depth")])
    xg_out, asked, mine, *dy_parts = pl.pallas_call(
        send_xg_kernel,
        out_shape=(hbm(xg_type), hbm(asked_type), hbm(mine_type)) + (hbm(four_type),) * GROUP,
        in_specs=[SMEM] + [ANY] * 7,
        out_specs=(VMEM, SMEM, SMEM) + (VMEM,) * GROUP,
        compiler_params=PARAMS,
        scratch_shapes=[
            pltpu.SMEM(cols.shape, jnp.int32),
            pltpu.SMEM(cols.shape, jnp.int32),
            pltpu.SMEM(tile_count.shape, jnp.int32),
            pltpu.VMEM(cols.shape, jnp.int32),
            pltpu.VMEM(counts.shape, jnp.int32),
            pltpu.VMEM(node_feat.shape, bf16),
            pltpu.VMEM(grad_out.shape, bf16),
            pltpu.VMEM(adjacency.shape, bf16),
            [pltpu.VMEM((slots * feat, LANES), jnp.float32)] * (width // LANES),
            pltpu.VMEM(asked_type.shape, jnp.int32),
            pltpu.SemaphoreType.DMA((7,)),
            pltpu.SemaphoreType.DMA((LOADS,)),
            pltpu.SemaphoreType.DMA,
        ],
    )(own, far(cols), far(tile_row.T), far(tile_count), far(counts), node_feat, grad_out, adjacency)
    xg_in = exchange(xg_out, "rows")
    dy_parts = [swap(part, GROUP * step) for step, part in enumerate(dy_parts)]
    hg_out = pl.pallas_call(
        h_kernel,
        out_shape=hbm(hg_type),
        in_specs=[SMEM, SMEM, VMEM, VMEM, VMEM, VMEM],
        out_specs=HBM,
        compiler_params=PARAMS,
        scratch_shapes=[
            tiles,
            pltpu.VMEM((peers * slots, peers * row_tiles), bf16),
            pltpu.VMEM((peers * row_tiles, width), jnp.float32),
            pltpu.VMEM(hg_type.shape, bf16),
            pltpu.SemaphoreType.DMA((STORES,)),
        ],
    )(far(mine), far(asked), near(cols), near(counts), near(xg_in), near(adjacency))
    hg_in = exchange(hg_out, "rows")
    dy_parts = pl.pallas_call(
        turn_kernel,
        out_shape=(hbm(four_type),) * GROUP,
        in_specs=[SMEM] + [VMEM] * GROUP,
        out_specs=(VMEM,) * GROUP,
        compiler_params=PARAMS,
        cost_estimate=pl.CostEstimate(flops=int(5e10), bytes_accessed=0, transcendentals=0),
    )(own, *dy_parts)
    dy_parts = [swap(part, step) for step, part in enumerate(dy_parts)]
    z_part = pl.pallas_call(
        fill_kernel,
        out_shape=z_type,
        in_specs=[SMEM, VMEM],
        out_specs=VMEM,
        compiler_params=PARAMS,
    )(mine, near(xg_in))
    z_out = pl.pallas_call(
        join_kernel,
        out_shape=z_type,
        in_specs=[SMEM, VMEM, HBM],
        out_specs=HBM,
        compiler_params=PARAMS,
        input_output_aliases={2: 0},
        scratch_shapes=[
            pltpu.VMEM((hg_type.shape[0] * row_tiles * (width // LANES), LANES), jnp.float32),
            tiles,
            pltpu.SemaphoreType.DMA((slots * (width // LANES),)),
            pltpu.SemaphoreType.DMA((slots,)),
        ],
    )(mine, near(hg_in), z_part)
    z_out, *dy_parts = lax.optimization_barrier((z_out, *dy_parts))
    dy = pl.pallas_call(
        order_kernel,
        out_shape=slot_type,
        in_specs=[SMEM] + [VMEM] * GROUP,
        out_specs=VMEM,
        compiler_params=PARAMS,
    )(own, *dy_parts)
    z_in = exchange(z_out, "depth")
    result = jnp.einsum("qfa,qfb->ab", dy, z_in[:, 2], preferred_element_type=jnp.float32)
    result += jnp.einsum("qfa,qfb->ab", z_in[:, 0], z_in[:, 1], preferred_element_type=jnp.float32)
    count = lax.dynamic_index_in_dim(tile_count, own_index, 0, keepdims=False)
    return jnp.where(lax.axis_index("depth") < count, result, 0.0)[None, None]


def solution(mesh):
    in_specs = (P("depth", "rows"), P("depth", "rows"), P("rows", None, None), P(), P(), P())
    out_specs = P("rows", "depth", None, None)
    return jax.shard_map(body, mesh=mesh, in_specs=in_specs, out_specs=out_specs, check_vma=False)
```

```python
import jax
import jax.numpy as jnp
from jax import lax
from jax.experimental import pallas as pl
from jax.experimental.pallas import tpu as pltpu
from jax.sharding import PartitionSpec as P

PAIR_MOST = 2
LOADS = 2
STORES = 4
LANES = 128
GROUP = 4
SMEM = pl.BlockSpec(memory_space=pltpu.SMEM)
VMEM = pl.BlockSpec(memory_space=pltpu.VMEM)
ANY = pl.BlockSpec(memory_space=pl.ANY)
HBM = pl.BlockSpec(memory_space=pltpu.HBM)
PARAMS = pltpu.CompilerParams(vmem_limit_bytes=12 * 2**20)


def tile_cols(index, width):
    return pl.ds(pl.multiple_of(index * width, width), width)


def send_xg_kernel(
    col_hbm, row_hbm, count_hbm, counts_hbm, x_hbm, dy_hbm, a_hbm,
    out_ref, asked_ref, mine_ref, dy0_ref, dy1_ref, dy2_ref, dy3_ref,
    col_ref, row_ref, count_ref, cols_ref, counts_ref, x_ref, dy_ref,
    a_ref, term_ref, code_ref, load_sem, a_sem, code_sem,
):
    slots, width = a_ref.shape[0], a_ref.shape[1]
    peers, most = out_ref.shape[0], PAIR_MOST
    feat = x_ref.shape[0]
    row_tiles = x_ref.shape[1] // width
    small = [
        pltpu.make_async_copy(source, target, load_sem.at[k])
        for k, (source, target) in enumerate(
            (
                (col_hbm, cols_ref),
                (counts_hbm, counts_ref),
                (col_hbm, col_ref),
                (row_hbm, row_ref),
                (count_hbm, count_ref),
                (dy_hbm, dy_ref),
                (x_hbm, x_ref),
            )
        )
    ]
    for load in small:
        load.start()
    loads = []
    for c in range(LOADS):
        part = pl.ds(c * (slots // LOADS), slots // LOADS)
        loads.append(pltpu.make_async_copy(a_hbm.at[part], a_ref.at[part], a_sem.at[c]))
        loads[c].start()
    own = lax.axis_index("rows")
    for load in small[:2]:
        load.wait()
    cols = cols_ref[...]
    slot_ids = lax.broadcasted_iota(jnp.int32, cols.shape, 0)
    wanted = (slot_ids < counts_ref[...]) & (cols // row_tiles == own)
    code = cols % row_tiles + 1
    first = jnp.max(jnp.where(wanted, (slots - 1 - slot_ids) * 8 + code, 0), axis=0, keepdims=True)
    last = jnp.max(jnp.where(wanted, slot_ids * 8 + code, 0), axis=0, keepdims=True)
    two = first // 8 + last // 8 != slots - 1
    code_ref[0:1] = first % 8
    code_ref[1:2] = jnp.where(two, last % 8, 0)
    to_scalars = pltpu.make_async_copy(code_ref, asked_ref, code_sem)
    to_scalars.start()
    for load in small[2:]:
        load.wait()
    owners = [col_ref[s, own] // row_tiles for s in range(slots)]
    for s in range(slots):
        row = row_ref[s, own]
        rank = jnp.int32(0)
        for earlier in range(s):
            rank = rank + jnp.where(owners[earlier] == owners[s], 1, 0)
        mine_ref[s] = jnp.where(s < count_ref[own], owners[s] * most + rank, -1)
        mine_ref[slots + s] = row
    for step, part_ref in enumerate((dy0_ref, dy1_ref, dy2_ref, dy3_ref)):
        group = lax.axis_index("depth") // GROUP ^ step
        for e in range(GROUP):
            part_ref[e] = dy_ref[:, tile_cols(row_ref[group * GROUP + e, own], width)]
    to_scalars.wait()
    for r in range(peers):
        for k in range(most):
            t = jnp.maximum(asked_ref[k, r] - 1, 0)
            out_ref[r, k * feat : (k + 1) * feat] = x_ref[:, tile_cols(t, width)]
    for s in range(slots):
        if s % (slots // LOADS) == 0:
            loads[s // (slots // LOADS)].wait()
        dy = dy_ref[:, tile_cols(mine_ref[slots + s], width)]
        term = jnp.dot(dy, a_ref[s], preferred_element_type=jnp.float32)
        for lanes, half in enumerate(term_ref):
            half[s * feat : (s + 1) * feat] = term[:, lanes * LANES : (lanes + 1) * LANES]
    for r in range(peers):
        for lanes, half in enumerate(term_ref):
            of_feature = half[pl.ds(r, slots, stride=feat)].astype(out_ref.dtype)
            out_ref[r, most * feat :, lanes * LANES : (lanes + 1) * LANES] = of_feature


def h_kernel(
    mine_ref, asked_ref, cols_ref, counts_ref, in_ref, a_ref,
    out_hbm, acc_ref, pick_ref, sum_ref, out_ref, out_sem,
):
    slots = a_ref.shape[0]
    peers, most = out_ref.shape[0], PAIR_MOST
    row_tiles, feat, width = acc_ref.shape
    sums = [jnp.zeros((feat, width), jnp.float32) for _ in range(row_tiles)]
    for s in range(slots):
        held = jnp.maximum(mine_ref[s], 0)
        row = mine_ref[slots + s]
        x = in_ref[held // most, pl.ds(pl.multiple_of(held % most * feat, feat), feat)]
        term = lax.dot_general(x, a_ref[s], (((1,), (1,)), ((), ())), preferred_element_type=jnp.float32)
        for t in range(row_tiles):
            sums[t] = sums[t] + jnp.where((row == t) & (mine_ref[s] >= 0), term, 0.0)
    for t in range(row_tiles):
        acc_ref[t] = sums[t].astype(acc_ref.dtype)
    cols = cols_ref[...]
    live = lax.broadcasted_iota(jnp.int32, cols.shape, 0) < counts_ref[...]
    cols = jnp.where(live, cols, -1)
    tile_ids = lax.broadcasted_iota(jnp.int32, (slots, peers * row_tiles), 1)
    for r in range(peers):
        pick_ref[r * slots : (r + 1) * slots] = (cols[:, r : r + 1] == tile_ids).astype(pick_ref.dtype)
    terms = in_ref[:, most * feat :].reshape(peers * slots, width)
    sum_ref[...] = lax.dot_general(
        pick_ref[...], terms, (((0,), (0,)), ((), ())), preferred_element_type=jnp.float32
    )
    stores = []
    for r in range(peers):
        of_tiles = sum_ref[r * row_tiles : (r + 1) * row_tiles]
        halves = []
        for half in range(width // LANES):
            lanes = slice(half * LANES, (half + 1) * LANES)
            for k in range(most):
                first = (half * most + k) * feat
                out_ref[r, first : first + feat] = acc_ref[jnp.maximum(asked_ref[k, r] - 1, 0), :, lanes]
            halves.append(of_tiles[:, lanes])
        out_ref[r, width // LANES * most * feat :] = jnp.concatenate(halves).astype(out_ref.dtype)
        if (r + 1) % (peers // STORES) == 0:
            part = pl.ds(r + 1 - peers // STORES, peers // STORES)
            copy = pltpu.make_async_copy(out_ref.at[part], out_hbm.at[part], out_sem.at[len(stores)])
            copy.start()
            stores.append(copy)
    for copy in stores:
        copy.wait()


def turn_kernel(in0_ref, in1_ref, in2_ref, in3_ref, out0_ref, out1_ref, out2_ref, out3_ref):
    for e, out_ref in enumerate((out0_ref, out1_ref, out2_ref, out3_ref)):
        for g, in_ref in enumerate((in0_ref, in1_ref, in2_ref, in3_ref)):
            out_ref[g] = in_ref[lax.axis_index("depth") % GROUP ^ e]


def order_kernel(in0_ref, in1_ref, in2_ref, in3_ref, out_ref):
    for e, in_ref in enumerate((in0_ref, in1_ref, in2_ref, in3_ref)):
        for g in range(GROUP):
            out_ref[lax.axis_index("depth") ^ (g * GROUP + e)] = in_ref[g]


def fill_kernel(mine_ref, in_ref, z_ref):
    slots, _, feat, _ = z_ref.shape
    for s in range(slots):
        held = jnp.maximum(mine_ref[s], 0)
        z_ref[s, 1] = in_ref[held // PAIR_MOST, pl.ds(pl.multiple_of(held % PAIR_MOST * feat, feat), feat)]


def join_kernel(mine_ref, in_ref, part_ref, z_ref, rows_ref, g_ref, h_sem, g_sem):
    del part_ref
    peers, most = in_ref.shape[0], PAIR_MOST
    slots = z_ref.shape[0]
    row_tiles, feat, width = g_ref.shape
    halves = width // LANES
    copies = []
    for s in range(slots):
        held = jnp.maximum(mine_ref[s], 0)
        for half in range(halves):
            first = pl.multiple_of((half * most + held % most) * feat, feat)
            tile = in_ref.at[held // most, pl.ds(first, feat)]
            place = z_ref.at[s, 2, :, pl.ds(half * LANES, LANES)]
            copies.append(pltpu.make_async_copy(tile, place, h_sem.at[s * halves + half]))
            copies[-1].start()
    step = halves * row_tiles
    for r in range(peers):
        rows_ref[r * step : (r + 1) * step] = in_ref[r, halves * most * feat :].astype(jnp.float32)
    for t in range(row_tiles):
        for half in range(halves):
            of_tile = rows_ref[pl.ds(half * row_tiles + t, feat, stride=step)].astype(g_ref.dtype)
            g_ref[t, :, half * LANES : (half + 1) * LANES] = of_tile
    for s in range(slots):
        copies.append(pltpu.make_async_copy(g_ref.at[mine_ref[slots + s]], z_ref.at[s, 0], g_sem.at[s]))
        copies[-1].start()
    for copy in copies:
        copy.wait()


def exchange(value, axis):
    return lax.all_to_all(value, axis, 0, 0, tiled=True)


def swap(value, step):
    if step == 0:
        return value
    places = range(lax.axis_size("depth"))
    return lax.ppermute(value, "depth", [(place, place ^ step) for place in places])


def hbm(kind):
    return pltpu.HBM(kind.shape, kind.dtype)


def far(value):
    return pltpu.with_memory_space_constraint(value, pltpu.HBM)


def near(value):
    return pltpu.with_memory_space_constraint(value, pltpu.VMEM)


def body(node_feat, grad_out, adjacency, tile_count, tile_row, tile_col):
    slots, width = adjacency.shape[0], adjacency.shape[1]
    feat = node_feat.shape[0]
    row_tiles = node_feat.shape[1] // width
    own_index = lax.axis_index("rows")
    peers = lax.axis_size("rows")
    bf16 = node_feat.dtype
    wanted_rows = PAIR_MOST * feat
    xg_type = jax.ShapeDtypeStruct((peers, wanted_rows + slots, width), bf16)
    hg_type = jax.ShapeDtypeStruct((peers, (wanted_rows + row_tiles) * (width // LANES), LANES), bf16)
    asked_type = jax.ShapeDtypeStruct((PAIR_MOST, peers), jnp.int32)
    mine_type = jax.ShapeDtypeStruct((2 * slots,), jnp.int32)
    z_type = jax.ShapeDtypeStruct((slots, 3, feat, width), bf16)
    tiles = pltpu.VMEM((row_tiles, feat, width), bf16)
    slot_type = jax.ShapeDtypeStruct((slots, feat, width), bf16)
    node_feat, grad_out, adjacency = far(node_feat), far(grad_out), far(adjacency)
    cols, counts = tile_col.T, tile_count[None]

    four_type = jax.ShapeDtypeStruct((GROUP, feat, width), bf16)
    xg_out, asked, mine, *dy_parts = pl.pallas_call(
        send_xg_kernel,
        out_shape=(hbm(xg_type), hbm(asked_type), hbm(mine_type)) + (hbm(four_type),) * GROUP,
        in_specs=[ANY] * 7,
        out_specs=(VMEM, SMEM, SMEM) + (VMEM,) * GROUP,
        compiler_params=PARAMS,
        scratch_shapes=[
            pltpu.SMEM(cols.shape, jnp.int32),
            pltpu.SMEM(cols.shape, jnp.int32),
            pltpu.SMEM(tile_count.shape, jnp.int32),
            pltpu.VMEM(cols.shape, jnp.int32),
            pltpu.VMEM(counts.shape, jnp.int32),
            pltpu.VMEM(node_feat.shape, bf16),
            pltpu.VMEM(grad_out.shape, bf16),
            pltpu.VMEM(adjacency.shape, bf16),
            [pltpu.VMEM((slots * feat, LANES), jnp.float32)] * (width // LANES),
            pltpu.VMEM(asked_type.shape, jnp.int32),
            pltpu.SemaphoreType.DMA((7,)),
            pltpu.SemaphoreType.DMA((LOADS,)),
            pltpu.SemaphoreType.DMA,
        ],
    )(far(cols), far(tile_row.T), far(tile_count), far(counts), node_feat, grad_out, adjacency)
    xg_in = exchange(xg_out, "rows")
    dy_parts = [swap(part, GROUP * step) for step, part in enumerate(dy_parts)]
    hg_out = pl.pallas_call(
        h_kernel,
        out_shape=hbm(hg_type),
        in_specs=[SMEM, SMEM, VMEM, VMEM, VMEM, VMEM],
        out_specs=HBM,
        compiler_params=PARAMS,
        scratch_shapes=[
            tiles,
            pltpu.VMEM((peers * slots, peers * row_tiles), bf16),
            pltpu.VMEM((peers * row_tiles, width), jnp.float32),
            pltpu.VMEM(hg_type.shape, bf16),
            pltpu.SemaphoreType.DMA((STORES,)),
        ],
    )(far(mine), far(asked), near(cols), near(counts), near(xg_in), near(adjacency))
    hg_in = exchange(hg_out, "rows")
    dy_parts = pl.pallas_call(
        turn_kernel,
        out_shape=(hbm(four_type),) * GROUP,
        in_specs=[VMEM] * GROUP,
        out_specs=(VMEM,) * GROUP,
        compiler_params=PARAMS,
        cost_estimate=pl.CostEstimate(flops=int(5e10), bytes_accessed=0, transcendentals=0),
    )(*dy_parts)
    dy_parts = [swap(part, step) for step, part in enumerate(dy_parts)]
    z_part = pl.pallas_call(
        fill_kernel,
        out_shape=z_type,
        in_specs=[SMEM, VMEM],
        out_specs=VMEM,
        compiler_params=PARAMS,
    )(mine, near(xg_in))
    z_out = pl.pallas_call(
        join_kernel,
        out_shape=z_type,
        in_specs=[SMEM, VMEM, HBM],
        out_specs=HBM,
        compiler_params=PARAMS,
        input_output_aliases={2: 0},
        scratch_shapes=[
            pltpu.VMEM((hg_type.shape[0] * row_tiles * (width // LANES), LANES), jnp.float32),
            tiles,
            pltpu.SemaphoreType.DMA((slots * (width // LANES),)),
            pltpu.SemaphoreType.DMA((slots,)),
        ],
    )(mine, near(hg_in), z_part)
    z_out, *dy_parts = lax.optimization_barrier((z_out, *dy_parts))
    dy = pl.pallas_call(
        order_kernel,
        out_shape=slot_type,
        in_specs=[VMEM] * GROUP,
        out_specs=VMEM,
        compiler_params=PARAMS,
    )(*dy_parts)
    z_in = exchange(z_out, "depth")
    result = jnp.einsum("qfa,qfb->ab", dy, z_in[:, 2], preferred_element_type=jnp.float32)
    result += jnp.einsum("qfa,qfb->ab", z_in[:, 0], z_in[:, 1], preferred_element_type=jnp.float32)
    count = lax.dynamic_index_in_dim(tile_count, own_index, 0, keepdims=False)
    return jnp.where(lax.axis_index("depth") < count, result, 0.0)[None, None]


def solution(mesh):
    in_specs = (P("depth", "rows"), P("depth", "rows"), P("rows", None, None), P(), P(), P())
    out_specs = P("rows", "depth", None, None)
    return jax.shard_map(body, mesh=mesh, in_specs=in_specs, out_specs=out_specs, check_vma=False)
```

```python
import jax
import jax.numpy as jnp
from jax import lax
from jax.experimental import pallas as pl
from jax.experimental.pallas import tpu as pltpu
from jax.sharding import PartitionSpec as P

PAIR_MOST = 2
LOADS = 2
STORES = 4
LANES = 128
GROUP = 4
SMEM = pl.BlockSpec(memory_space=pltpu.SMEM)
VMEM = pl.BlockSpec(memory_space=pltpu.VMEM)
ANY = pl.BlockSpec(memory_space=pl.ANY)
HBM = pl.BlockSpec(memory_space=pltpu.HBM)
PARAMS = pltpu.CompilerParams(vmem_limit_bytes=12 * 2**20)


def tile_cols(index, width):
    return pl.ds(pl.multiple_of(index * width, width), width)


def send_xg_kernel(
    col_hbm, row_hbm, count_hbm, counts_hbm, x_hbm, dy_hbm, a_hbm,
    out_ref, asked_ref, mine_ref, dy0_ref, dy1_ref, dy2_ref, dy3_ref,
    col_ref, row_ref, count_ref, cols_ref, counts_ref, x_ref, dy_ref,
    a_ref, term_ref, code_ref, load_sem, a_sem, code_sem,
):
    slots, width = a_ref.shape[0], a_ref.shape[1]
    peers, most = out_ref.shape[0], PAIR_MOST
    feat = x_ref.shape[0]
    row_tiles = x_ref.shape[1] // width
    small = [
        pltpu.make_async_copy(source, target, load_sem.at[k])
        for k, (source, target) in enumerate(
            (
                (col_hbm, cols_ref),
                (counts_hbm, counts_ref),
                (col_hbm, col_ref),
                (row_hbm, row_ref),
                (count_hbm, count_ref),
                (dy_hbm, dy_ref),
                (x_hbm, x_ref),
            )
        )
    ]
    for load in small:
        load.start()
    loads = []
    for c in range(LOADS):
        part = pl.ds(c * (slots // LOADS), slots // LOADS)
        loads.append(pltpu.make_async_copy(a_hbm.at[part], a_ref.at[part], a_sem.at[c]))
        loads[c].start()
    own = lax.axis_index("rows")
    for load in small[:2]:
        load.wait()
    cols = cols_ref[...]
    slot_ids = lax.broadcasted_iota(jnp.int32, cols.shape, 0)
    wanted = (slot_ids < counts_ref[...]) & (cols // row_tiles == own)
    code = cols % row_tiles + 1
    first = jnp.max(jnp.where(wanted, (slots - 1 - slot_ids) * 8 + code, 0), axis=0, keepdims=True)
    last = jnp.max(jnp.where(wanted, slot_ids * 8 + code, 0), axis=0, keepdims=True)
    two = first // 8 + last // 8 != slots - 1
    code_ref[0:1] = first % 8
    code_ref[1:2] = jnp.where(two, last % 8, 0)
    to_scalars = pltpu.make_async_copy(code_ref, asked_ref, code_sem)
    to_scalars.start()
    for load in small[2:]:
        load.wait()
    owners = [col_ref[s, own] // row_tiles for s in range(slots)]
    for s in range(slots):
        row = row_ref[s, own]
        rank = jnp.int32(0)
        for earlier in range(s):
            rank = rank + jnp.where(owners[earlier] == owners[s], 1, 0)
        mine_ref[s] = jnp.where(s < count_ref[own], owners[s] * most + rank, -1)
        mine_ref[slots + s] = row
    for step, part_ref in enumerate((dy0_ref, dy1_ref, dy2_ref, dy3_ref)):
        group = lax.axis_index("depth") // GROUP ^ step
        for e in range(GROUP):
            part_ref[e] = dy_ref[:, tile_cols(row_ref[group * GROUP + e, own], width)]
    to_scalars.wait()
    for r in range(peers):
        for k in range(most):
            t = jnp.maximum(asked_ref[k, r] - 1, 0)
            out_ref[r, k * feat : (k + 1) * feat] = x_ref[:, tile_cols(t, width)]
    for s in range(slots):
        if s % (slots // LOADS) == 0:
            loads[s // (slots // LOADS)].wait()
        dy = dy_ref[:, tile_cols(mine_ref[slots + s], width)]
        term = jnp.dot(dy, a_ref[s], preferred_element_type=jnp.float32)
        for lanes, half in enumerate(term_ref):
            half[s * feat : (s + 1) * feat] = term[:, lanes * LANES : (lanes + 1) * LANES]
    for r in range(peers):
        for lanes, half in enumerate(term_ref):
            of_feature = half[pl.ds(r, slots, stride=feat)].astype(out_ref.dtype)
            out_ref[r, most * feat :, lanes * LANES : (lanes + 1) * LANES] = of_feature


def h_kernel(
    mine_hbm, asked_hbm, cols_ref, counts_ref, in_ref, a_ref,
    out_hbm, mine_ref, asked_ref, acc_ref, pick_ref, sum_ref, out_ref, small_sem, out_sem,
):
    slots = a_ref.shape[0]
    peers, most = out_ref.shape[0], PAIR_MOST
    row_tiles, feat, width = acc_ref.shape
    small = [
        pltpu.make_async_copy(mine_hbm, mine_ref, small_sem.at[0]),
        pltpu.make_async_copy(asked_hbm, asked_ref, small_sem.at[1]),
    ]
    for load in small:
        load.start()
    cols = cols_ref[...]
    live = lax.broadcasted_iota(jnp.int32, cols.shape, 0) < counts_ref[...]
    cols = jnp.where(live, cols, -1)
    tile_ids = lax.broadcasted_iota(jnp.int32, (slots, peers * row_tiles), 1)
    for r in range(peers):
        pick_ref[r * slots : (r + 1) * slots] = (cols[:, r : r + 1] == tile_ids).astype(pick_ref.dtype)
    terms = in_ref[:, most * feat :].reshape(peers * slots, width)
    sum_ref[...] = lax.dot_general(
        pick_ref[...], terms, (((0,), (0,)), ((), ())), preferred_element_type=jnp.float32
    )
    for load in small:
        load.wait()
    sums = [jnp.zeros((feat, width), jnp.float32) for _ in range(row_tiles)]
    for s in range(slots):
        held = jnp.maximum(mine_ref[s], 0)
        row = mine_ref[slots + s]
        x = in_ref[held // most, pl.ds(pl.multiple_of(held % most * feat, feat), feat)]
        term = lax.dot_general(x, a_ref[s], (((1,), (1,)), ((), ())), preferred_element_type=jnp.float32)
        for t in range(row_tiles):
            sums[t] = sums[t] + jnp.where((row == t) & (mine_ref[s] >= 0), term, 0.0)
    for t in range(row_tiles):
        acc_ref[t] = sums[t].astype(acc_ref.dtype)
    stores = []
    for r in range(peers):
        of_tiles = sum_ref[r * row_tiles : (r + 1) * row_tiles]
        halves = []
        for half in range(width // LANES):
            lanes = slice(half * LANES, (half + 1) * LANES)
            for k in range(most):
                first = (half * most + k) * feat
                out_ref[r, first : first + feat] = acc_ref[jnp.maximum(asked_ref[k, r] - 1, 0), :, lanes]
            halves.append(of_tiles[:, lanes])
        out_ref[r, width // LANES * most * feat :] = jnp.concatenate(halves).astype(out_ref.dtype)
        if (r + 1) % (peers // STORES) == 0:
            part = pl.ds(r + 1 - peers // STORES, peers // STORES)
            copy = pltpu.make_async_copy(out_ref.at[part], out_hbm.at[part], out_sem.at[len(stores)])
            copy.start()
            stores.append(copy)
    for copy in stores:
        copy.wait()


def turn_kernel(in0_ref, in1_ref, in2_ref, in3_ref, out0_ref, out1_ref, out2_ref, out3_ref):
    for e, out_ref in enumerate((out0_ref, out1_ref, out2_ref, out3_ref)):
        for g, in_ref in enumerate((in0_ref, in1_ref, in2_ref, in3_ref)):
            out_ref[g] = in_ref[lax.axis_index("depth") % GROUP ^ e]


def order_kernel(in0_ref, in1_ref, in2_ref, in3_ref, out_ref):
    for e, in_ref in enumerate((in0_ref, in1_ref, in2_ref, in3_ref)):
        for g in range(GROUP):
            out_ref[lax.axis_index("depth") ^ (g * GROUP + e)] = in_ref[g]


def fill_kernel(mine_ref, in_ref, z_ref):
    slots, _, feat, _ = z_ref.shape
    for s in range(slots):
        held = jnp.maximum(mine_ref[s], 0)
        z_ref[s, 1] = in_ref[held // PAIR_MOST, pl.ds(pl.multiple_of(held % PAIR_MOST * feat, feat), feat)]


def join_kernel(mine_hbm, in_ref, part_ref, z_ref, mine_ref, rows_ref, g_ref, mine_sem, h_sem, g_sem):
    del part_ref
    peers, most = in_ref.shape[0], PAIR_MOST
    slots = z_ref.shape[0]
    row_tiles, feat, width = g_ref.shape
    halves = width // LANES
    load = pltpu.make_async_copy(mine_hbm, mine_ref, mine_sem)
    load.start()
    step = halves * row_tiles
    for r in range(peers):
        rows_ref[r * step : (r + 1) * step] = in_ref[r, halves * most * feat :].astype(jnp.float32)
    for t in range(row_tiles):
        for half in range(halves):
            of_tile = rows_ref[pl.ds(half * row_tiles + t, feat, stride=step)].astype(g_ref.dtype)
            g_ref[t, :, half * LANES : (half + 1) * LANES] = of_tile
    load.wait()
    copies = []
    for s in range(slots):
        held = jnp.maximum(mine_ref[s], 0)
        for half in range(halves):
            first = pl.multiple_of((half * most + held % most) * feat, feat)
            tile = in_ref.at[held // most, pl.ds(first, feat)]
            place = z_ref.at[s, 2, :, pl.ds(half * LANES, LANES)]
            copies.append(pltpu.make_async_copy(tile, place, h_sem.at[s * halves + half]))
            copies[-1].start()
    for s in range(slots):
        copies.append(pltpu.make_async_copy(g_ref.at[mine_ref[slots + s]], z_ref.at[s, 0], g_sem.at[s]))
        copies[-1].start()
    for copy in copies:
        copy.wait()


def exchange(value, axis):
    return lax.all_to_all(value, axis, 0, 0, tiled=True)


def swap(value, step):
    if step == 0:
        return value
    places = range(lax.axis_size("depth"))
    return lax.ppermute(value, "depth", [(place, place ^ step) for place in places])


def hbm(kind):
    return pltpu.HBM(kind.shape, kind.dtype)


def far(value):
    return pltpu.with_memory_space_constraint(value, pltpu.HBM)


def near(value):
    return pltpu.with_memory_space_constraint(value, pltpu.VMEM)


def body(node_feat, grad_out, adjacency, tile_count, tile_row, tile_col):
    slots, width = adjacency.shape[0], adjacency.shape[1]
    feat = node_feat.shape[0]
    row_tiles = node_feat.shape[1] // width
    own_index = lax.axis_index("rows")
    peers = lax.axis_size("rows")
    bf16 = node_feat.dtype
    wanted_rows = PAIR_MOST * feat
    xg_type = jax.ShapeDtypeStruct((peers, wanted_rows + slots, width), bf16)
    hg_type = jax.ShapeDtypeStruct((peers, (wanted_rows + row_tiles) * (width // LANES), LANES), bf16)
    asked_type = jax.ShapeDtypeStruct((PAIR_MOST, peers), jnp.int32)
    mine_type = jax.ShapeDtypeStruct((2 * slots,), jnp.int32)
    z_type = jax.ShapeDtypeStruct((slots, 3, feat, width), bf16)
    tiles = pltpu.VMEM((row_tiles, feat, width), bf16)
    slot_type = jax.ShapeDtypeStruct((slots, feat, width), bf16)
    node_feat, grad_out, adjacency = far(node_feat), far(grad_out), far(adjacency)
    cols, counts = tile_col.T, tile_count[None]

    four_type = jax.ShapeDtypeStruct((GROUP, feat, width), bf16)
    xg_out, asked, mine, *dy_parts = pl.pallas_call(
        send_xg_kernel,
        out_shape=(hbm(xg_type), hbm(asked_type), hbm(mine_type)) + (hbm(four_type),) * GROUP,
        in_specs=[ANY] * 7,
        out_specs=(VMEM, SMEM, SMEM) + (VMEM,) * GROUP,
        compiler_params=PARAMS,
        scratch_shapes=[
            pltpu.SMEM(cols.shape, jnp.int32),
            pltpu.SMEM(cols.shape, jnp.int32),
            pltpu.SMEM(tile_count.shape, jnp.int32),
            pltpu.VMEM(cols.shape, jnp.int32),
            pltpu.VMEM(counts.shape, jnp.int32),
            pltpu.VMEM(node_feat.shape, bf16),
            pltpu.VMEM(grad_out.shape, bf16),
            pltpu.VMEM(adjacency.shape, bf16),
            [pltpu.VMEM((slots * feat, LANES), jnp.float32)] * (width // LANES),
            pltpu.VMEM(asked_type.shape, jnp.int32),
            pltpu.SemaphoreType.DMA((7,)),
            pltpu.SemaphoreType.DMA((LOADS,)),
            pltpu.SemaphoreType.DMA,
        ],
    )(far(cols), far(tile_row.T), far(tile_count), far(counts), node_feat, grad_out, adjacency)
    xg_in = exchange(xg_out, "rows")
    dy_parts = [swap(part, GROUP * step) for step, part in enumerate(dy_parts)]
    hg_out = pl.pallas_call(
        h_kernel,
        out_shape=hbm(hg_type),
        in_specs=[ANY, ANY, VMEM, VMEM, VMEM, VMEM],
        out_specs=HBM,
        compiler_params=PARAMS,
        scratch_shapes=[
            pltpu.SMEM(mine_type.shape, jnp.int32),
            pltpu.SMEM(asked_type.shape, jnp.int32),
            tiles,
            pltpu.VMEM((peers * slots, peers * row_tiles), bf16),
            pltpu.VMEM((peers * row_tiles, width), jnp.float32),
            pltpu.VMEM(hg_type.shape, bf16),
            pltpu.SemaphoreType.DMA((2,)),
            pltpu.SemaphoreType.DMA((STORES,)),
        ],
    )(far(mine), far(asked), near(cols), near(counts), near(xg_in), near(adjacency))
    hg_in = exchange(hg_out, "rows")
    dy_parts = pl.pallas_call(
        turn_kernel,
        out_shape=(hbm(four_type),) * GROUP,
        in_specs=[VMEM] * GROUP,
        out_specs=(VMEM,) * GROUP,
        compiler_params=PARAMS,
        cost_estimate=pl.CostEstimate(flops=int(5e10), bytes_accessed=0, transcendentals=0),
    )(*dy_parts)
    dy_parts = [swap(part, step) for step, part in enumerate(dy_parts)]
    z_part = pl.pallas_call(
        fill_kernel,
        out_shape=z_type,
        in_specs=[SMEM, VMEM],
        out_specs=VMEM,
        compiler_params=PARAMS,
    )(mine, near(xg_in))
    z_out = pl.pallas_call(
        join_kernel,
        out_shape=z_type,
        in_specs=[ANY, VMEM, HBM],
        out_specs=HBM,
        compiler_params=PARAMS,
        input_output_aliases={2: 0},
        scratch_shapes=[
            pltpu.SMEM(mine_type.shape, jnp.int32),
            pltpu.VMEM((hg_type.shape[0] * row_tiles * (width // LANES), LANES), jnp.float32),
            tiles,
            pltpu.SemaphoreType.DMA,
            pltpu.SemaphoreType.DMA((slots * (width // LANES),)),
            pltpu.SemaphoreType.DMA((slots,)),
        ],
    )(far(mine), near(hg_in), z_part)
    z_out, *dy_parts = lax.optimization_barrier((z_out, *dy_parts))
    dy = pl.pallas_call(
        order_kernel,
        out_shape=slot_type,
        in_specs=[VMEM] * GROUP,
        out_specs=VMEM,
        compiler_params=PARAMS,
    )(*dy_parts)
    z_in = exchange(z_out, "depth")
    result = jnp.einsum("qfa,qfb->ab", dy, z_in[:, 2], preferred_element_type=jnp.float32)
    result += jnp.einsum("qfa,qfb->ab", z_in[:, 0], z_in[:, 1], preferred_element_type=jnp.float32)
    count = lax.dynamic_index_in_dim(tile_count, own_index, 0, keepdims=False)
    return jnp.where(lax.axis_index("depth") < count, result, 0.0)[None, None]


def solution(mesh):
    in_specs = (P("depth", "rows"), P("depth", "rows"), P("rows", None, None), P(), P(), P())
    out_specs = P("rows", "depth", None, None)
    return jax.shard_map(body, mesh=mesh, in_specs=in_specs, out_specs=out_specs, check_vma=False)
```

```python
import jax
import jax.numpy as jnp
from jax import lax
from jax.experimental import pallas as pl
from jax.experimental.pallas import tpu as pltpu
from jax.sharding import PartitionSpec as P

PAIR_MOST = 2
LOADS = 2
STORES = 4
LANES = 128
GROUP = 4
ORDER = (0, 2, 1, 3)
SMEM = pl.BlockSpec(memory_space=pltpu.SMEM)
VMEM = pl.BlockSpec(memory_space=pltpu.VMEM)
ANY = pl.BlockSpec(memory_space=pl.ANY)
HBM = pl.BlockSpec(memory_space=pltpu.HBM)
PARAMS = pltpu.CompilerParams(vmem_limit_bytes=12 * 2**20)


def tile_cols(index, width):
    return pl.ds(pl.multiple_of(index * width, width), width)


def send_xg_kernel(
    col_hbm, row_hbm, count_hbm, counts_hbm, x_hbm, dy_hbm, a_hbm,
    out_ref, asked_ref, mine_ref, dy0_ref, dy1_ref, dy2_ref, dy3_ref,
    col_ref, row_ref, count_ref, cols_ref, counts_ref, x_ref, dy_ref,
    a_ref, term_ref, code_ref, load_sem, a_sem, code_sem,
):
    slots, width = a_ref.shape[0], a_ref.shape[1]
    peers, most = out_ref.shape[0], PAIR_MOST
    feat = x_ref.shape[0]
    row_tiles = x_ref.shape[1] // width
    small = [
        pltpu.make_async_copy(source, target, load_sem.at[k])
        for k, (source, target) in enumerate(
            (
                (col_hbm, cols_ref),
                (counts_hbm, counts_ref),
                (col_hbm, col_ref),
                (row_hbm, row_ref),
                (count_hbm, count_ref),
                (dy_hbm, dy_ref),
                (x_hbm, x_ref),
            )
        )
    ]
    for load in small:
        load.start()
    loads = []
    for c in range(LOADS):
        part = pl.ds(c * (slots // LOADS), slots // LOADS)
        loads.append(pltpu.make_async_copy(a_hbm.at[part], a_ref.at[part], a_sem.at[c]))
        loads[c].start()
    own = lax.axis_index("rows")
    for load in small[:2]:
        load.wait()
    cols = cols_ref[...]
    slot_ids = lax.broadcasted_iota(jnp.int32, cols.shape, 0)
    wanted = (slot_ids < counts_ref[...]) & (cols // row_tiles == own)
    code = cols % row_tiles + 1
    first = jnp.max(jnp.where(wanted, (slots - 1 - slot_ids) * 8 + code, 0), axis=0, keepdims=True)
    last = jnp.max(jnp.where(wanted, slot_ids * 8 + code, 0), axis=0, keepdims=True)
    two = first // 8 + last // 8 != slots - 1
    code_ref[0:1] = first % 8
    code_ref[1:2] = jnp.where(two, last % 8, 0)
    to_scalars = pltpu.make_async_copy(code_ref, asked_ref, code_sem)
    to_scalars.start()
    for load in small[2:]:
        load.wait()
    owners = [col_ref[s, own] // row_tiles for s in range(slots)]
    for s in range(slots):
        row = row_ref[s, own]
        rank = jnp.int32(0)
        for earlier in range(s):
            rank = rank + jnp.where(owners[earlier] == owners[s], 1, 0)
        mine_ref[s] = jnp.where(s < count_ref[own], owners[s] * most + rank, -1)
        mine_ref[slots + s] = row
    for step, part_ref in enumerate((dy0_ref, dy1_ref, dy2_ref, dy3_ref)):
        group = lax.axis_index("depth") // GROUP ^ step
        for e in range(GROUP):
            part_ref[e] = dy_ref[:, tile_cols(row_ref[group * GROUP + e, own], width)]
    to_scalars.wait()
    for r in range(peers):
        for k in range(most):
            t = jnp.maximum(asked_ref[k, r] - 1, 0)
            out_ref[r, k * feat : (k + 1) * feat] = x_ref[:, tile_cols(t, width)]
    for s in range(slots):
        if s % (slots // LOADS) == 0:
            loads[s // (slots // LOADS)].wait()
        dy = dy_ref[:, tile_cols(mine_ref[slots + s], width)]
        term = jnp.dot(dy, a_ref[s], preferred_element_type=jnp.float32)
        for lanes, half in enumerate(term_ref):
            half[s * feat : (s + 1) * feat] = term[:, lanes * LANES : (lanes + 1) * LANES]
    for r in range(peers):
        for lanes, half in enumerate(term_ref):
            of_feature = half[pl.ds(r, slots, stride=feat)].astype(out_ref.dtype)
            out_ref[r, most * feat :, lanes * LANES : (lanes + 1) * LANES] = of_feature


def h_kernel(
    mine_hbm, asked_hbm, cols_ref, counts_ref, in_ref, a_ref,
    out_hbm, mine_ref, asked_ref, acc_ref, pick_ref, sum_ref, out_ref, small_sem, out_sem,
):
    slots = a_ref.shape[0]
    peers, most = out_ref.shape[0], PAIR_MOST
    row_tiles, feat, width = acc_ref.shape
    small = [
        pltpu.make_async_copy(mine_hbm, mine_ref, small_sem.at[0]),
        pltpu.make_async_copy(asked_hbm, asked_ref, small_sem.at[1]),
    ]
    for load in small:
        load.start()
    cols = cols_ref[...]
    live = lax.broadcasted_iota(jnp.int32, cols.shape, 0) < counts_ref[...]
    cols = jnp.where(live, cols, -1)
    tile_ids = lax.broadcasted_iota(jnp.int32, (slots, peers * row_tiles), 1)
    for r in range(peers):
        pick_ref[r * slots : (r + 1) * slots] = (cols[:, r : r + 1] == tile_ids).astype(pick_ref.dtype)
    terms = in_ref[:, most * feat :].reshape(peers * slots, width)
    sum_ref[...] = lax.dot_general(
        pick_ref[...], terms, (((0,), (0,)), ((), ())), preferred_element_type=jnp.float32
    )
    for load in small:
        load.wait()
    sums = [jnp.zeros((feat, width), jnp.float32) for _ in range(row_tiles)]
    for s in range(slots):
        held = jnp.maximum(mine_ref[s], 0)
        row = mine_ref[slots + s]
        x = in_ref[held // most, pl.ds(pl.multiple_of(held % most * feat, feat), feat)]
        term = lax.dot_general(x, a_ref[s], (((1,), (1,)), ((), ())), preferred_element_type=jnp.float32)
        for t in range(row_tiles):
            sums[t] = sums[t] + jnp.where((row == t) & (mine_ref[s] >= 0), term, 0.0)
    for t in range(row_tiles):
        acc_ref[t] = sums[t].astype(acc_ref.dtype)
    stores = []
    for r in range(peers):
        of_tiles = sum_ref[r * row_tiles : (r + 1) * row_tiles]
        halves = []
        for half in range(width // LANES):
            lanes = slice(half * LANES, (half + 1) * LANES)
            for k in range(most):
                first = (half * most + k) * feat
                out_ref[r, first : first + feat] = acc_ref[jnp.maximum(asked_ref[k, r] - 1, 0), :, lanes]
            halves.append(of_tiles[:, lanes])
        out_ref[r, width // LANES * most * feat :] = jnp.concatenate(halves).astype(out_ref.dtype)
        if (r + 1) % (peers // STORES) == 0:
            part = pl.ds(r + 1 - peers // STORES, peers // STORES)
            copy = pltpu.make_async_copy(out_ref.at[part], out_hbm.at[part], out_sem.at[len(stores)])
            copy.start()
            stores.append(copy)
    for copy in stores:
        copy.wait()


def turn_kernel(in0_ref, in1_ref, in2_ref, in3_ref, out0_ref, out1_ref, out2_ref, out3_ref):
    for e, out_ref in enumerate((out0_ref, out1_ref, out2_ref, out3_ref)):
        for g, in_ref in zip(ORDER, (in0_ref, in1_ref, in2_ref, in3_ref)):
            out_ref[g] = in_ref[lax.axis_index("depth") % GROUP ^ e]


def order_kernel(in0_ref, in1_ref, in2_ref, in3_ref, out_ref):
    for e, in_ref in enumerate((in0_ref, in1_ref, in2_ref, in3_ref)):
        for g in range(GROUP):
            out_ref[lax.axis_index("depth") ^ (g * GROUP + e)] = in_ref[g]


def fill_kernel(mine_ref, in_ref, z_ref):
    slots, _, feat, _ = z_ref.shape
    for s in range(slots):
        held = jnp.maximum(mine_ref[s], 0)
        z_ref[s, 1] = in_ref[held // PAIR_MOST, pl.ds(pl.multiple_of(held % PAIR_MOST * feat, feat), feat)]


def join_kernel(mine_hbm, in_ref, part_ref, z_ref, mine_ref, rows_ref, g_ref, mine_sem, h_sem, g_sem):
    del part_ref
    peers, most = in_ref.shape[0], PAIR_MOST
    slots = z_ref.shape[0]
    row_tiles, feat, width = g_ref.shape
    halves = width // LANES
    load = pltpu.make_async_copy(mine_hbm, mine_ref, mine_sem)
    load.start()
    step = halves * row_tiles
    for r in range(peers):
        rows_ref[r * step : (r + 1) * step] = in_ref[r, halves * most * feat :].astype(jnp.float32)
    for t in range(row_tiles):
        for half in range(halves):
            of_tile = rows_ref[pl.ds(half * row_tiles + t, feat, stride=step)].astype(g_ref.dtype)
            g_ref[t, :, half * LANES : (half + 1) * LANES] = of_tile
    load.wait()
    copies = []
    for s in range(slots):
        held = jnp.maximum(mine_ref[s], 0)
        for half in range(halves):
            first = pl.multiple_of((half * most + held % most) * feat, feat)
            tile = in_ref.at[held // most, pl.ds(first, feat)]
            place = z_ref.at[s, 2, :, pl.ds(half * LANES, LANES)]
            copies.append(pltpu.make_async_copy(tile, place, h_sem.at[s * halves + half]))
            copies[-1].start()
    for s in range(slots):
        copies.append(pltpu.make_async_copy(g_ref.at[mine_ref[slots + s]], z_ref.at[s, 0], g_sem.at[s]))
        copies[-1].start()
    for copy in copies:
        copy.wait()


def exchange(value, axis):
    return lax.all_to_all(value, axis, 0, 0, tiled=True)


def swap(value, step):
    if step == 0:
        return value
    places = range(lax.axis_size("depth"))
    return lax.ppermute(value, "depth", [(place, place ^ step) for place in places])


def hbm(kind):
    return pltpu.HBM(kind.shape, kind.dtype)


def far(value):
    return pltpu.with_memory_space_constraint(value, pltpu.HBM)


def near(value):
    return pltpu.with_memory_space_constraint(value, pltpu.VMEM)


def body(node_feat, grad_out, adjacency, tile_count, tile_row, tile_col):
    slots, width = adjacency.shape[0], adjacency.shape[1]
    feat = node_feat.shape[0]
    row_tiles = node_feat.shape[1] // width
    own_index = lax.axis_index("rows")
    peers = lax.axis_size("rows")
    bf16 = node_feat.dtype
    wanted_rows = PAIR_MOST * feat
    xg_type = jax.ShapeDtypeStruct((peers, wanted_rows + slots, width), bf16)
    hg_type = jax.ShapeDtypeStruct((peers, (wanted_rows + row_tiles) * (width // LANES), LANES), bf16)
    asked_type = jax.ShapeDtypeStruct((PAIR_MOST, peers), jnp.int32)
    mine_type = jax.ShapeDtypeStruct((2 * slots,), jnp.int32)
    z_type = jax.ShapeDtypeStruct((slots, 3, feat, width), bf16)
    tiles = pltpu.VMEM((row_tiles, feat, width), bf16)
    slot_type = jax.ShapeDtypeStruct((slots, feat, width), bf16)
    node_feat, grad_out, adjacency = far(node_feat), far(grad_out), far(adjacency)
    cols, counts = tile_col.T, tile_count[None]

    four_type = jax.ShapeDtypeStruct((GROUP, feat, width), bf16)
    xg_out, asked, mine, *dy_parts = pl.pallas_call(
        send_xg_kernel,
        out_shape=(hbm(xg_type), hbm(asked_type), hbm(mine_type)) + (hbm(four_type),) * GROUP,
        in_specs=[ANY] * 7,
        out_specs=(VMEM, SMEM, SMEM) + (VMEM,) * GROUP,
        compiler_params=PARAMS,
        scratch_shapes=[
            pltpu.SMEM(cols.shape, jnp.int32),
            pltpu.SMEM(cols.shape, jnp.int32),
            pltpu.SMEM(tile_count.shape, jnp.int32),
            pltpu.VMEM(cols.shape, jnp.int32),
            pltpu.VMEM(counts.shape, jnp.int32),
            pltpu.VMEM(node_feat.shape, bf16),
            pltpu.VMEM(grad_out.shape, bf16),
            pltpu.VMEM(adjacency.shape, bf16),
            [pltpu.VMEM((slots * feat, LANES), jnp.float32)] * (width // LANES),
            pltpu.VMEM(asked_type.shape, jnp.int32),
            pltpu.SemaphoreType.DMA((7,)),
            pltpu.SemaphoreType.DMA((LOADS,)),
            pltpu.SemaphoreType.DMA,
        ],
    )(far(cols), far(tile_row.T), far(tile_count), far(counts), node_feat, grad_out, adjacency)
    xg_in = exchange(xg_out, "rows")
    dy_parts = [swap(dy_parts[step], GROUP * step) for step in ORDER]
    hg_out = pl.pallas_call(
        h_kernel,
        out_shape=hbm(hg_type),
        in_specs=[ANY, ANY, VMEM, VMEM, VMEM, VMEM],
        out_specs=HBM,
        compiler_params=PARAMS,
        scratch_shapes=[
            pltpu.SMEM(mine_type.shape, jnp.int32),
            pltpu.SMEM(asked_type.shape, jnp.int32),
            tiles,
            pltpu.VMEM((peers * slots, peers * row_tiles), bf16),
            pltpu.VMEM((peers * row_tiles, width), jnp.float32),
            pltpu.VMEM(hg_type.shape, bf16),
            pltpu.SemaphoreType.DMA((2,)),
            pltpu.SemaphoreType.DMA((STORES,)),
        ],
    )(far(mine), far(asked), near(cols), near(counts), near(xg_in), near(adjacency))
    hg_in = exchange(hg_out, "rows")
    dy_parts = pl.pallas_call(
        turn_kernel,
        out_shape=(hbm(four_type),) * GROUP,
        in_specs=[VMEM] * GROUP,
        out_specs=(VMEM,) * GROUP,
        compiler_params=PARAMS,
        cost_estimate=pl.CostEstimate(flops=int(5e10), bytes_accessed=0, transcendentals=0),
    )(*dy_parts)
    dy_parts = [swap(part, step) for step, part in enumerate(dy_parts)]
    z_part = pl.pallas_call(
        fill_kernel,
        out_shape=z_type,
        in_specs=[SMEM, VMEM],
        out_specs=VMEM,
        compiler_params=PARAMS,
    )(mine, near(xg_in))
    z_out = pl.pallas_call(
        join_kernel,
        out_shape=z_type,
        in_specs=[ANY, VMEM, HBM],
        out_specs=HBM,
        compiler_params=PARAMS,
        input_output_aliases={2: 0},
        scratch_shapes=[
            pltpu.SMEM(mine_type.shape, jnp.int32),
            pltpu.VMEM((hg_type.shape[0] * row_tiles * (width // LANES), LANES), jnp.float32),
            tiles,
            pltpu.SemaphoreType.DMA,
            pltpu.SemaphoreType.DMA((slots * (width // LANES),)),
            pltpu.SemaphoreType.DMA((slots,)),
        ],
    )(far(mine), near(hg_in), z_part)
    z_out, *dy_parts = lax.optimization_barrier((z_out, *dy_parts))
    dy = pl.pallas_call(
        order_kernel,
        out_shape=slot_type,
        in_specs=[VMEM] * GROUP,
        out_specs=VMEM,
        compiler_params=PARAMS,
    )(*dy_parts)
    z_in = exchange(z_out, "depth")
    result = jnp.einsum("qfa,qfb->ab", dy, z_in[:, 2], preferred_element_type=jnp.float32)
    result += jnp.einsum("qfa,qfb->ab", z_in[:, 0], z_in[:, 1], preferred_element_type=jnp.float32)
    count = lax.dynamic_index_in_dim(tile_count, own_index, 0, keepdims=False)
    return jnp.where(lax.axis_index("depth") < count, result, 0.0)[None, None]


def solution(mesh):
    in_specs = (P("depth", "rows"), P("depth", "rows"), P("rows", None, None), P(), P(), P())
    out_specs = P("rows", "depth", None, None)
    return jax.shard_map(body, mesh=mesh, in_specs=in_specs, out_specs=out_specs, check_vma=False)
```

```python
import jax
import jax.numpy as jnp
from jax import lax
from jax.experimental import pallas as pl
from jax.experimental.pallas import tpu as pltpu
from jax.sharding import PartitionSpec as P

PAIR_MOST = 2
LOADS = 2
STORES = 2
LANES = 128
GROUP = 4
SMEM = pl.BlockSpec(memory_space=pltpu.SMEM)
VMEM = pl.BlockSpec(memory_space=pltpu.VMEM)
ANY = pl.BlockSpec(memory_space=pl.ANY)
HBM = pl.BlockSpec(memory_space=pltpu.HBM)
PARAMS = pltpu.CompilerParams(vmem_limit_bytes=12 * 2**20)


def tile_cols(index, width):
    return pl.ds(pl.multiple_of(index * width, width), width)


def send_xg_kernel(
    col_hbm, row_hbm, count_hbm, counts_hbm, x_hbm, dy_hbm, a_hbm,
    out_ref, asked_ref, mine_ref, dy0_ref, dy1_ref, dy2_ref, dy3_ref,
    col_ref, row_ref, count_ref, cols_ref, counts_ref, x_ref, dy_ref,
    a_ref, term_ref, code_ref, load_sem, a_sem, code_sem,
):
    slots, width = a_ref.shape[0], a_ref.shape[1]
    peers, most = out_ref.shape[0], PAIR_MOST
    feat = x_ref.shape[0]
    row_tiles = x_ref.shape[1] // width
    small = [
        pltpu.make_async_copy(source, target, load_sem.at[k])
        for k, (source, target) in enumerate(
            (
                (col_hbm, cols_ref),
                (counts_hbm, counts_ref),
                (col_hbm, col_ref),
                (row_hbm, row_ref),
                (count_hbm, count_ref),
                (dy_hbm, dy_ref),
                (x_hbm, x_ref),
            )
        )
    ]
    for load in small:
        load.start()
    loads = []
    for c in range(LOADS):
        part = pl.ds(c * (slots // LOADS), slots // LOADS)
        loads.append(pltpu.make_async_copy(a_hbm.at[part], a_ref.at[part], a_sem.at[c]))
        loads[c].start()
    own = lax.axis_index("rows")
    for load in small[:2]:
        load.wait()
    cols = cols_ref[...]
    slot_ids = lax.broadcasted_iota(jnp.int32, cols.shape, 0)
    wanted = (slot_ids < counts_ref[...]) & (cols // row_tiles == own)
    code = cols % row_tiles + 1
    first = jnp.max(jnp.where(wanted, (slots - 1 - slot_ids) * 8 + code, 0), axis=0, keepdims=True)
    last = jnp.max(jnp.where(wanted, slot_ids * 8 + code, 0), axis=0, keepdims=True)
    two = first // 8 + last // 8 != slots - 1
    code_ref[0:1] = first % 8
    code_ref[1:2] = jnp.where(two, last % 8, 0)
    to_scalars = pltpu.make_async_copy(code_ref, asked_ref, code_sem)
    to_scalars.start()
    for load in small[2:]:
        load.wait()
    owners = [col_ref[s, own] // row_tiles for s in range(slots)]
    for s in range(slots):
        row = row_ref[s, own]
        rank = jnp.int32(0)
        for earlier in range(s):
            rank = rank + jnp.where(owners[earlier] == owners[s], 1, 0)
        mine_ref[s] = jnp.where(s < count_ref[own], owners[s] * most + rank, -1)
        mine_ref[slots + s] = row
    for step, part_ref in enumerate((dy0_ref, dy1_ref, dy2_ref, dy3_ref)):
        group = lax.axis_index("depth") // GROUP ^ step
        for e in range(GROUP):
            part_ref[e] = dy_ref[:, tile_cols(row_ref[group * GROUP + e, own], width)]
    to_scalars.wait()
    for r in range(peers):
        for k in range(most):
            t = jnp.maximum(asked_ref[k, r] - 1, 0)
            out_ref[r, k * feat : (k + 1) * feat] = x_ref[:, tile_cols(t, width)]
    for s in range(slots):
        if s % (slots // LOADS) == 0:
            loads[s // (slots // LOADS)].wait()
        dy = dy_ref[:, tile_cols(mine_ref[slots + s], width)]
        term = jnp.dot(dy, a_ref[s], preferred_element_type=jnp.float32)
        for lanes, half in enumerate(term_ref):
            half[s * feat : (s + 1) * feat] = term[:, lanes * LANES : (lanes + 1) * LANES]
    for r in range(peers):
        for lanes, half in enumerate(term_ref):
            of_feature = half[pl.ds(r, slots, stride=feat)].astype(out_ref.dtype)
            out_ref[r, most * feat :, lanes * LANES : (lanes + 1) * LANES] = of_feature


def h_kernel(
    mine_hbm, asked_hbm, cols_ref, counts_ref, in_ref, a_ref,
    out_hbm, mine_ref, asked_ref, acc_ref, pick_ref, sum_ref, out_ref, small_sem, out_sem,
):
    slots = a_ref.shape[0]
    peers, most = out_ref.shape[0], PAIR_MOST
    row_tiles, feat, width = acc_ref.shape
    small = [
        pltpu.make_async_copy(mine_hbm, mine_ref, small_sem.at[0]),
        pltpu.make_async_copy(asked_hbm, asked_ref, small_sem.at[1]),
    ]
    for load in small:
        load.start()
    cols = cols_ref[...]
    live = lax.broadcasted_iota(jnp.int32, cols.shape, 0) < counts_ref[...]
    cols = jnp.where(live, cols, -1)
    tile_ids = lax.broadcasted_iota(jnp.int32, (slots, peers * row_tiles), 1)
    for r in range(peers):
        pick_ref[r * slots : (r + 1) * slots] = (cols[:, r : r + 1] == tile_ids).astype(pick_ref.dtype)
    terms = in_ref[:, most * feat :].reshape(peers * slots, width)
    sum_ref[...] = lax.dot_general(
        pick_ref[...], terms, (((0,), (0,)), ((), ())), preferred_element_type=jnp.float32
    )
    for load in small:
        load.wait()
    sums = [jnp.zeros((feat, width), jnp.float32) for _ in range(row_tiles)]
    for s in range(slots):
        held = jnp.maximum(mine_ref[s], 0)
        row = mine_ref[slots + s]
        x = in_ref[held // most, pl.ds(pl.multiple_of(held % most * feat, feat), feat)]
        term = lax.dot_general(x, a_ref[s], (((1,), (1,)), ((), ())), preferred_element_type=jnp.float32)
        for t in range(row_tiles):
            sums[t] = sums[t] + jnp.where((row == t) & (mine_ref[s] >= 0), term, 0.0)
    for t in range(row_tiles):
        acc_ref[t] = sums[t].astype(acc_ref.dtype)
    stores = []
    for r in range(peers):
        of_tiles = sum_ref[r * row_tiles : (r + 1) * row_tiles]
        halves = []
        for half in range(width // LANES):
            lanes = slice(half * LANES, (half + 1) * LANES)
            for k in range(most):
                first = (half * most + k) * feat
                out_ref[r, first : first + feat] = acc_ref[jnp.maximum(asked_ref[k, r] - 1, 0), :, lanes]
            halves.append(of_tiles[:, lanes])
        out_ref[r, width // LANES * most * feat :] = jnp.concatenate(halves).astype(out_ref.dtype)
        if (r + 1) % (peers // STORES) == 0:
            part = pl.ds(r + 1 - peers // STORES, peers // STORES)
            copy = pltpu.make_async_copy(out_ref.at[part], out_hbm.at[part], out_sem.at[len(stores)])
            copy.start()
            stores.append(copy)
    for copy in stores:
        copy.wait()


def turn_kernel(in0_ref, in1_ref, in2_ref, in3_ref, out0_ref, out1_ref, out2_ref, out3_ref):
    for e, out_ref in enumerate((out0_ref, out1_ref, out2_ref, out3_ref)):
        for g, in_ref in enumerate((in0_ref, in1_ref, in2_ref, in3_ref)):
            out_ref[g] = in_ref[lax.axis_index("depth") % GROUP ^ e]


def order_kernel(in0_ref, in1_ref, in2_ref, in3_ref, out_ref):
    for e, in_ref in enumerate((in0_ref, in1_ref, in2_ref, in3_ref)):
        for g in range(GROUP):
            out_ref[lax.axis_index("depth") ^ (g * GROUP + e)] = in_ref[g]


def fill_kernel(mine_ref, in_ref, z_ref):
    slots, _, feat, _ = z_ref.shape
    for s in range(slots):
        held = jnp.maximum(mine_ref[s], 0)
        z_ref[s, 1] = in_ref[held // PAIR_MOST, pl.ds(pl.multiple_of(held % PAIR_MOST * feat, feat), feat)]


def join_kernel(mine_hbm, in_ref, part_ref, z_ref, mine_ref, rows_ref, g_ref, mine_sem, h_sem, g_sem):
    del part_ref
    peers, most = in_ref.shape[0], PAIR_MOST
    slots = z_ref.shape[0]
    row_tiles, feat, width = g_ref.shape
    halves = width // LANES
    load = pltpu.make_async_copy(mine_hbm, mine_ref, mine_sem)
    load.start()
    step = halves * row_tiles
    for r in range(peers):
        rows_ref[r * step : (r + 1) * step] = in_ref[r, halves * most * feat :].astype(jnp.float32)
    for t in range(row_tiles):
        for half in range(halves):
            of_tile = rows_ref[pl.ds(half * row_tiles + t, feat, stride=step)].astype(g_ref.dtype)
            g_ref[t, :, half * LANES : (half + 1) * LANES] = of_tile
    load.wait()
    copies = []
    for s in range(slots):
        held = jnp.maximum(mine_ref[s], 0)
        for half in range(halves):
            first = pl.multiple_of((half * most + held % most) * feat, feat)
            tile = in_ref.at[held // most, pl.ds(first, feat)]
            place = z_ref.at[s, 2, :, pl.ds(half * LANES, LANES)]
            copies.append(pltpu.make_async_copy(tile, place, h_sem.at[s * halves + half]))
            copies[-1].start()
    for s in range(slots):
        copies.append(pltpu.make_async_copy(g_ref.at[mine_ref[slots + s]], z_ref.at[s, 0], g_sem.at[s]))
        copies[-1].start()
    for copy in copies:
        copy.wait()


def exchange(value, axis):
    return lax.all_to_all(value, axis, 0, 0, tiled=True)


def swap(value, step):
    if step == 0:
        return value
    places = range(lax.axis_size("depth"))
    return lax.ppermute(value, "depth", [(place, place ^ step) for place in places])


def hbm(kind):
    return pltpu.HBM(kind.shape, kind.dtype)


def far(value):
    return pltpu.with_memory_space_constraint(value, pltpu.HBM)


def near(value):
    return pltpu.with_memory_space_constraint(value, pltpu.VMEM)


def body(node_feat, grad_out, adjacency, tile_count, tile_row, tile_col):
    slots, width = adjacency.shape[0], adjacency.shape[1]
    feat = node_feat.shape[0]
    row_tiles = node_feat.shape[1] // width
    own_index = lax.axis_index("rows")
    peers = lax.axis_size("rows")
    bf16 = node_feat.dtype
    wanted_rows = PAIR_MOST * feat
    xg_type = jax.ShapeDtypeStruct((peers, wanted_rows + slots, width), bf16)
    hg_type = jax.ShapeDtypeStruct((peers, (wanted_rows + row_tiles) * (width // LANES), LANES), bf16)
    asked_type = jax.ShapeDtypeStruct((PAIR_MOST, peers), jnp.int32)
    mine_type = jax.ShapeDtypeStruct((2 * slots,), jnp.int32)
    z_type = jax.ShapeDtypeStruct((slots, 3, feat, width), bf16)
    tiles = pltpu.VMEM((row_tiles, feat, width), bf16)
    slot_type = jax.ShapeDtypeStruct((slots, feat, width), bf16)
    node_feat, grad_out, adjacency = far(node_feat), far(grad_out), far(adjacency)
    cols, counts = tile_col.T, tile_count[None]

    four_type = jax.ShapeDtypeStruct((GROUP, feat, width), bf16)
    xg_out, asked, mine, *dy_parts = pl.pallas_call(
        send_xg_kernel,
        out_shape=(hbm(xg_type), hbm(asked_type), hbm(mine_type)) + (hbm(four_type),) * GROUP,
        in_specs=[ANY] * 7,
        out_specs=(VMEM, SMEM, SMEM) + (VMEM,) * GROUP,
        compiler_params=PARAMS,
        scratch_shapes=[
            pltpu.SMEM(cols.shape, jnp.int32),
            pltpu.SMEM(cols.shape, jnp.int32),
            pltpu.SMEM(tile_count.shape, jnp.int32),
            pltpu.VMEM(cols.shape, jnp.int32),
            pltpu.VMEM(counts.shape, jnp.int32),
            pltpu.VMEM(node_feat.shape, bf16),
            pltpu.VMEM(grad_out.shape, bf16),
            pltpu.VMEM(adjacency.shape, bf16),
            [pltpu.VMEM((slots * feat, LANES), jnp.float32)] * (width // LANES),
            pltpu.VMEM(asked_type.shape, jnp.int32),
            pltpu.SemaphoreType.DMA((7,)),
            pltpu.SemaphoreType.DMA((LOADS,)),
            pltpu.SemaphoreType.DMA,
        ],
    )(far(cols), far(tile_row.T), far(tile_count), far(counts), node_feat, grad_out, adjacency)
    xg_in = exchange(xg_out, "rows")
    dy_parts = [swap(part, GROUP * step) for step, part in enumerate(dy_parts)]
    hg_out = pl.pallas_call(
        h_kernel,
        out_shape=hbm(hg_type),
        in_specs=[ANY, ANY, VMEM, VMEM, VMEM, VMEM],
        out_specs=HBM,
        compiler_params=PARAMS,
        scratch_shapes=[
            pltpu.SMEM(mine_type.shape, jnp.int32),
            pltpu.SMEM(asked_type.shape, jnp.int32),
            tiles,
            pltpu.VMEM((peers * slots, peers * row_tiles), bf16),
            pltpu.VMEM((peers * row_tiles, width), jnp.float32),
            pltpu.VMEM(hg_type.shape, bf16),
            pltpu.SemaphoreType.DMA((2,)),
            pltpu.SemaphoreType.DMA((STORES,)),
        ],
    )(far(mine), far(asked), near(cols), near(counts), near(xg_in), near(adjacency))
    hg_in = exchange(hg_out, "rows")
    dy_parts = pl.pallas_call(
        turn_kernel,
        out_shape=(hbm(four_type),) * GROUP,
        in_specs=[VMEM] * GROUP,
        out_specs=(VMEM,) * GROUP,
        compiler_params=PARAMS,
        cost_estimate=pl.CostEstimate(flops=int(5e10), bytes_accessed=0, transcendentals=0),
    )(*dy_parts)
    dy_parts = [swap(part, step) for step, part in enumerate(dy_parts)]
    z_part = pl.pallas_call(
        fill_kernel,
        out_shape=z_type,
        in_specs=[SMEM, VMEM],
        out_specs=VMEM,
        compiler_params=PARAMS,
    )(mine, near(xg_in))
    z_out = pl.pallas_call(
        join_kernel,
        out_shape=z_type,
        in_specs=[ANY, VMEM, HBM],
        out_specs=HBM,
        compiler_params=PARAMS,
        input_output_aliases={2: 0},
        scratch_shapes=[
            pltpu.SMEM(mine_type.shape, jnp.int32),
            pltpu.VMEM((hg_type.shape[0] * row_tiles * (width // LANES), LANES), jnp.float32),
            tiles,
            pltpu.SemaphoreType.DMA,
            pltpu.SemaphoreType.DMA((slots * (width // LANES),)),
            pltpu.SemaphoreType.DMA((slots,)),
        ],
    )(far(mine), near(hg_in), z_part)
    z_out, *dy_parts = lax.optimization_barrier((z_out, *dy_parts))
    dy = pl.pallas_call(
        order_kernel,
        out_shape=slot_type,
        in_specs=[VMEM] * GROUP,
        out_specs=VMEM,
        compiler_params=PARAMS,
    )(*dy_parts)
    z_in = exchange(z_out, "depth")
    result = jnp.einsum("qfa,qfb->ab", dy, z_in[:, 2], preferred_element_type=jnp.float32)
    result += jnp.einsum("qfa,qfb->ab", z_in[:, 0], z_in[:, 1], preferred_element_type=jnp.float32)
    count = lax.dynamic_index_in_dim(tile_count, own_index, 0, keepdims=False)
    return jnp.where(lax.axis_index("depth") < count, result, 0.0)[None, None]


def solution(mesh):
    in_specs = (P("depth", "rows"), P("depth", "rows"), P("rows", None, None), P(), P(), P())
    out_specs = P("rows", "depth", None, None)
    return jax.shard_map(body, mesh=mesh, in_specs=in_specs, out_specs=out_specs, check_vma=False)
```
